32 devices in a mesh: seq: 8 (over z, y), batch: 4 (over x, core).
Axes of the slice: x: 2, y: 2, z: 4, core: 2. Of those that a mesh axis runs over, the one named last changes fastest.
Arguments:
- residual_in: bfloat16 [4, 2048, 1536], P('batch', 'seq'), may hold values from -6 to 6
- seg_ids: int32 [4, 2048], P('batch', 'seq'), may hold values from 0 to 10, as said below
- doc_starts: int32 [4, 12], P('batch'), may hold values from 0 to 2048, as said below
- norm_gain: bfloat16 [1536], P(('seq', 'batch')), may hold values from 0.5 to 1.5
- in_weight: bfloat16 [1536, 6448], P(('seq', 'batch')), may hold values from -0.15625 to 0.15625
- conv_weight: bfloat16 [3328, 4], P(('seq', 'batch')), may hold values from -3 to 3
- conv_bias: bfloat16 [3328], P(('seq', 'batch')), may hold values from -3 to 3
- dt_bias: float32 [48], replicated, may hold values from -7 to -1
- a_log: float32 [48], replicated, may hold values from 0 to 1.5
- skip_weight: float32 [48], replicated, may hold values from 0.5 to 1.5
- gate_gain: bfloat16 [3072], P(('seq', 'batch')), may hold values from 0.5 to 1.5
- out_weight: bfloat16 [3072, 1536], P(('seq', 'batch')), may hold values from -0.109375 to 0.109375
- cotangent: bfloat16 [4, 2048, 1536], P('batch', 'seq'), may hold values from -6 to 6
Outputs:
- mixed_out: bfloat16 [4, 2048, 1536], P('batch', 'seq')
- input_grad: float32 [4, 2048, 1536], P('batch', 'seq')
- norm_gain_grad: float32 [1536], P(('seq', 'batch'))
- in_weight_grad: float32 [1536, 6448], P(('seq', 'batch'))
- conv_weight_grad: float32 [3328, 4], P(('seq', 'batch'))
- conv_bias_grad: float32 [3328], P(('seq', 'batch'))
- dt_bias_grad: float32 [48], replicated
- a_log_grad: float32 [48], replicated
- skip_weight_grad: float32 [48], replicated
- gate_gain_grad: float32 [3072], P(('seq', 'batch'))
- out_weight_grad: float32 [3072, 1536], P(('seq', 'batch'))
The draws below stay inside these ranges and needn't reach their ends.
Inputs may be any that keep to these rules, and one draw needn't show every extreme that they name: `doc_starts`: each row starts with 0; entries below 2048 rise by 200 to 2000 from one to the next; all later entries equal 2048. seg_ids at a position is the number of entries of its sequence's doc_starts at or below that position, minus one.
All inputs are finite; a program needn't handle non-finite values.
Results may differ from the reference program's by a relative error of at most 0.011.
Values may be sent and summed in bfloat16 or wider, within the bound.
No kernel may reach another device: no remote copies, remote signals or barrier semaphores. Data moves between devices by JAX's collectives and lax.ppermute only.
A program may use at most 256 MiB of HBM per device.

```python
import jax
import jax.numpy as jnp
from jax import lax

D = 1536
E = 3072
H = 48
P_SIZE = 64
N = 128
K = 4
GROUP = 256
DOC_MIN = 200
DOC_MAX = 2000
C = 3328
F_IN = 6448
LENGTH = 2048
SEQS = 4
MAXDOC = 12
N_SEQ = 8


def doc_layout(key):
    key_lengths = jax.random.fold_in(key, 7)
    key_first = jax.random.fold_in(key, 11)
    key_offset = jax.random.fold_in(key, 13)
    key_pick = jax.random.fold_in(key, 17)
    key_extra = jax.random.fold_in(key, 19)
    dense_count = LENGTH // DOC_MIN
    spare = (LENGTH - 1 - dense_count * DOC_MIN) // dense_count
    lengths = jax.random.randint(key_lengths, (SEQS, MAXDOC - 2), DOC_MIN, DOC_MAX + 1)
    first_two = jax.random.randint(key_first, (SEQS, 2), DOC_MIN + GROUP, DOC_MIN + 2 * GROUP + 1)
    offsets = jax.random.randint(key_offset, (SEQS,), 1, K)
    start_one = first_two[:, 0] // GROUP * GROUP
    start_two = (start_one + first_two[:, 1]) // GROUP * GROUP + offsets
    later = start_two[:, None] + jnp.cumsum(lengths, axis=1) - lengths
    anchored = jnp.concatenate([jnp.zeros((SEQS, 1), jnp.int32), start_one[:, None].astype(jnp.int32), later.astype(jnp.int32)], axis=1)
    gaps = DOC_MIN + jax.random.randint(key_extra, (SEQS, MAXDOC), 0, spare + 1)
    dense = (jnp.cumsum(gaps, axis=1) - gaps).astype(jnp.int32)
    chosen = jax.random.randint(key_pick, (), 0, SEQS)
    row_ids = jnp.arange(SEQS, dtype=jnp.int32)
    merged = jnp.where(row_ids[:, None] == chosen, dense, anchored)
    return jnp.minimum(merged, LENGTH).astype(jnp.int32)


def draw_doc_starts(key, part):
    return doc_layout(key)


def draw_seg_ids(key, part):
    starts = doc_layout(key)
    places = jnp.arange(LENGTH, dtype=jnp.int32)
    counted = jnp.sum((starts[:, None, :] <= places[None, :, None]).astype(jnp.int32), axis=2)
    return (counted - 1).astype(jnp.int32)


def block_scale(stream_key, shape, cuts, smallest, top_value):
    def one(dim, blocks):
        draws = jax.random.uniform(jax.random.fold_in(jax.random.fold_in(stream_key, 6), dim), (blocks,), jnp.float32, smallest / len(cuts), top_value / len(cuts))
        return jnp.repeat(jnp.exp(draws), shape[dim] // blocks).reshape((-1,) + (1,) * (len(shape) - dim - 1))

    factor_of = one(*cuts[0])
    for cut in cuts[1:]:
        factor_of = factor_of * one(*cut)
    return factor_of


def scatter_about(rng, extent, scale, most, cuts=(), kind=jnp.bfloat16):
    factor_of = block_scale(rng, extent, cuts, -0.22, 0.18) if cuts else 1.0
    values = jax.random.normal(rng, extent, jnp.float32) * scale * factor_of
    return jnp.minimum(jnp.maximum(values, -most), most).astype(kind)


def setup_inputs(seed: int = 0) -> dict:
    key_of = jax.random.split(jax.random.key(seed), 14)
    residual_in = scatter_about(key_of[0], (SEQS, LENGTH, D), 1.0, 6.0, ((0, 4), (1, 8)))
    seg_ids = draw_seg_ids(jax.random.fold_in(key_of[13], 71), 0)
    doc_starts = draw_doc_starts(jax.random.fold_in(key_of[13], 71), 0)
    norm_gain = jnp.clip(1.0 + 0.1 * jax.random.normal(key_of[3], (D,), jnp.float32), 0.5, 1.5).astype(jnp.bfloat16)
    in_weight = scatter_about(key_of[4], (D, F_IN), D ** -0.5, 0.15625, ((0, 32),))
    conv_weight = scatter_about(key_of[5], (C, K), K ** -0.5, 3.0, ((0, 32),))
    conv_bias = scatter_about(key_of[6], (C,), 0.5, 3.0, ((0, 32),))
    dt_bias = jnp.clip(jax.random.uniform(key_of[7], (H,), jnp.float32, -7.0, -1.0), -7.0, -1.0)
    a_log = jnp.clip(jax.random.uniform(key_of[8], (H,), jnp.float32, 0.0, 1.5), 0.0, 1.5)
    skip_weight = jnp.clip(jax.random.uniform(key_of[9], (H,), jnp.float32, 0.5, 1.5), 0.5, 1.5)
    gate_gain = jnp.clip(1.0 + 0.1 * jax.random.normal(key_of[10], (E,), jnp.float32), 0.5, 1.5).astype(jnp.bfloat16)
    out_weight = scatter_about(key_of[11], (E, D), E ** -0.5, 0.109375, ((0, 32),))
    cotangent = scatter_about(key_of[12], (SEQS, LENGTH, D), 1.0, 6.0, ((0, 4), (1, 8)))
    return {"residual_in": residual_in, "seg_ids": seg_ids, "doc_starts": doc_starts, "norm_gain": norm_gain, "in_weight": in_weight, "conv_weight": conv_weight, "conv_bias": conv_bias, "dt_bias": dt_bias, "a_log": a_log, "skip_weight": skip_weight, "gate_gain": gate_gain, "out_weight": out_weight, "cotangent": cotangent}


highest = lax.Precision.HIGHEST
epsilon = 1e-05

def rms_scale(values, gain_vec):
    return values * lax.rsqrt(lax.optimization_barrier(jnp.mean(values * values, axis=-1, keepdims=True)) + epsilon) * gain_vec

def doc_index(starts, places):
    return lax.optimization_barrier(jnp.sum((starts[..., None, :] <= places[..., None]).astype(jnp.int32), axis=-1)) - 1

def conv_block(inputs, edge_rows, kernel, offset, seg_rows, doc_edge, doc_head):
    lead_taps = kernel.shape[1] - 1
    block_len = inputs.shape[1]
    lanes = inputs.shape[0]
    extended = jnp.concatenate([edge_rows, inputs], axis=1)
    running = offset + kernel[:, lead_taps] * inputs
    for shift_by in range(1, lead_taps + 1):
        source = extended[:, lead_taps - shift_by:lead_taps - shift_by + block_len]
        near_ids = jnp.concatenate([jnp.full((lanes, shift_by), -1, jnp.int32), seg_rows[:, :block_len - shift_by]], axis=1)
        near_same = seg_rows == near_ids
        far_same = doc_edge[:, lead_taps - shift_by:lead_taps] == doc_head[:, :shift_by]
        far_full = jnp.concatenate([far_same, jnp.zeros((lanes, block_len - shift_by), dtype=bool)], axis=1)
        weight_mask = jnp.where(near_same | far_full, 1.0, 0.0).astype(inputs.dtype)
        running = running + kernel[:, lead_taps - shift_by] * source * weight_mask[..., None]
    return running

def prep_block(projected, edge_rows, kernel, offset, bias_dt, alog_vec, seg_rows, doc_edge, doc_head):
    lanes = projected.shape[0]
    block_len = projected.shape[1]
    gate_part = projected[..., :E]
    conv_in = projected[..., E:E + C]
    dt_raw = projected[..., E + C:]
    activated = jax.nn.silu(conv_block(conv_in, edge_rows, kernel, offset, seg_rows, doc_edge, doc_head))
    heads_x = activated[..., :E].reshape(lanes, block_len, H, P_SIZE)
    b_rows = activated[..., E:E + N]
    c_rows = activated[..., E + N:]
    step_dt = jax.nn.softplus(dt_raw + bias_dt)
    rates = -jnp.exp(alog_vec) * step_dt
    return (gate_part, heads_x, b_rows, c_rows, step_dt, rates)

def block_state(heads_x, b_rows, step_dt, rates, seg_rows, begins_doc):
    cumulative = jnp.cumsum(rates, axis=1)
    last_cum = cumulative[:, -1:, :]
    in_tail = seg_rows == seg_rows[:, -1:]
    weights = jnp.where(in_tail[..., None], jnp.exp(last_cum - cumulative), 0.0) * step_dt
    scaled = heads_x * weights[..., None]
    end_state = jnp.einsum('bshp,bsn->bhpn', scaled, b_rows, precision=highest)
    whole_doc = (seg_rows[:, -1] == seg_rows[:, 0]) & jnp.logical_not(begins_doc)
    block_decay = jnp.where(whole_doc[:, None], jnp.exp(last_cum[:, 0, :]), 0.0)
    return (end_state, block_decay)

def block_output(heads_x, b_rows, c_rows, step_dt, rates, gate_part, seg_rows, begins_doc, state_in, skip_vec, gain_vec):
    lanes, block_len = seg_rows.shape
    cumulative = jnp.cumsum(rates, axis=1)
    cum_heads = jnp.swapaxes(cumulative, 1, 2)
    differences = cum_heads[:, :, :, None] - cum_heads[:, :, None, :]
    places = jnp.arange(block_len, dtype=jnp.int32)
    causal = places[:, None] >= places[None, :]
    same_doc = (seg_rows[:, :, None] == seg_rows[:, None, :]) & causal[None]
    decays = jnp.exp(jnp.where(same_doc[:, None], differences, -jnp.inf))
    scores = jnp.einsum('btn,bsn->bts', c_rows, b_rows, precision=highest)
    mixing = decays * scores[:, None]
    scaled = heads_x * step_dt[..., None]
    within = jnp.einsum('bhts,bshp->bthp', mixing, scaled, precision=highest)
    continues = (seg_rows == seg_rows[:, :1]) & jnp.logical_not(begins_doc)[:, None]
    entering = jnp.where(continues[..., None], jnp.exp(cumulative), 0.0)
    carried = jnp.einsum('btn,bhpn->bthp', c_rows, state_in, precision=highest) * entering[..., None]
    summed = within + carried + skip_vec[:, None] * heads_x
    gated_rows = summed.reshape(lanes, block_len, E) * jax.nn.silu(gate_part)
    return rms_scale(gated_rows, gain_vec)

def sequence_mixer(projected, kernel, offset, bias_dt, alog_vec, skip_vec, gain_vec, seg_row, starts):
    blocks = N_SEQ
    proj_blocks = projected.reshape(blocks, GROUP, F_IN)
    conv_in = proj_blocks[..., E:E + C]
    edge_rows = jnp.concatenate([jnp.zeros((1, K - 1, C), projected.dtype), conv_in[:-1, GROUP - K + 1:]], axis=0)
    block_start = jnp.arange(blocks, dtype=jnp.int32) * GROUP
    tap_places = jnp.arange(K - 1, dtype=jnp.int32)
    doc_edge = doc_index(starts[None, :], block_start[:, None] - (K - 1) + tap_places[None, :])
    doc_head = doc_index(starts[None, :], block_start[:, None] + tap_places[None, :])
    seg_rows = seg_row.reshape(blocks, GROUP)
    begins_doc = jnp.any(starts[None, :] == block_start[:, None], axis=1)
    gate_part, heads_x, b_rows, c_rows, step_dt, rates = prep_block(proj_blocks, edge_rows, kernel, offset, bias_dt, alog_vec, seg_rows, doc_edge, doc_head)
    end_state, block_decay = block_state(heads_x, b_rows, step_dt, rates, seg_rows, begins_doc)

    def advance(running, pieces):
        local_state, local_decay = pieces
        return (local_decay[:, None, None] * running + local_state, running)
    _, state_in = lax.scan(advance, jnp.zeros((H, P_SIZE, N), projected.dtype), (end_state, block_decay))
    result = block_output(heads_x, b_rows, c_rows, step_dt, rates, gate_part, seg_rows, begins_doc, state_in, skip_vec, gain_vec)
    return result.reshape(blocks * GROUP, E)

def reference(residual_in, seg_ids, doc_starts, norm_gain, in_weight, conv_weight, conv_bias, dt_bias, a_log, skip_weight, gate_gain, out_weight, cotangent):
    kernel = conv_weight.astype(jnp.float32)
    offset = conv_bias.astype(jnp.float32)
    gain_out = gate_gain.astype(jnp.float32)
    gain_in = norm_gain.astype(jnp.float32)

    def per_sequence(totals, pieces):
        rows_in, seg_row, starts, grad_rows = pieces
        resid_float = rows_in.astype(jnp.float32)
        normed, norm_back = jax.vjp(rms_scale, resid_float, gain_in)
        normed_low = normed.astype(jnp.bfloat16)
        projected = jnp.dot(normed_low, in_weight, preferred_element_type=jnp.float32).astype(jnp.bfloat16)

        def mixer_fn(proj_f, kern, offs, bias_dt, alog_vec, skip_vec, gain_vec):
            return sequence_mixer(proj_f, kern, offs, bias_dt, alog_vec, skip_vec, gain_vec, seg_row, starts)
        mixer_out, mix_back = jax.vjp(mixer_fn, projected.astype(jnp.float32), kernel, offset, dt_bias, a_log, skip_weight, gain_out)
        mixer_low = mixer_out.astype(jnp.bfloat16)
        mixed = (resid_float + jnp.dot(mixer_low, out_weight, preferred_element_type=jnp.float32)).astype(jnp.bfloat16)
        mixer_grad = jnp.dot(grad_rows, out_weight.T, preferred_element_type=jnp.float32)
        out_w_grad = jnp.dot(mixer_low.T, grad_rows, preferred_element_type=jnp.float32)
        proj_grad, kernel_grad, offset_grad, bias_grad, alog_grad, skip_grad, gain_grad = mix_back(mixer_grad)
        proj_low = proj_grad.astype(jnp.bfloat16)
        normed_grad = jnp.dot(proj_low, in_weight.T, preferred_element_type=jnp.float32)
        in_w_grad = jnp.dot(normed_low.T, proj_low, preferred_element_type=jnp.float32)
        resid_grad, norm_grad = norm_back(normed_grad)
        input_grad = grad_rows.astype(jnp.float32) + resid_grad
        terms = (norm_grad, in_w_grad, kernel_grad, offset_grad, bias_grad, alog_grad, skip_grad, gain_grad, out_w_grad)
        updated = tuple((total + term for total, term in zip(totals, terms)))
        return (updated, (mixed, input_grad))
    start_totals = (jnp.zeros((D,), jnp.float32), jnp.zeros((D, F_IN), jnp.float32), jnp.zeros((C, K), jnp.float32), jnp.zeros((C,), jnp.float32), jnp.zeros((H,), jnp.float32), jnp.zeros((H,), jnp.float32), jnp.zeros((H,), jnp.float32), jnp.zeros((E,), jnp.float32), jnp.zeros((E, D), jnp.float32))
    totals, stacked = lax.scan(per_sequence, start_totals, (residual_in, seg_ids, doc_starts, cotangent))
    mixed_out, input_grad = stacked
    return (mixed_out, input_grad, totals[0], totals[1], totals[2], totals[3], totals[4], totals[5], totals[6], totals[7], totals[8])
```

```python
import functools

import jax
import jax.numpy as jnp
from jax import lax
from jax.experimental import pallas as pl
from jax.experimental.pallas import tpu as pltpu
from jax.sharding import Mesh, PartitionSpec as P


f32 = jnp.float32
bf16 = jnp.bfloat16
highest = lax.Precision.HIGHEST
epsilon = 1e-05
HALO = 16
LANES = 128
MASKED = -1e30
INTERPRET = False
PLANE = ("lo", "bx", "core")
SWAP = ((0, 1), (1, 0))
CROSS = ((0, 3), (3, 0), (1, 2), (2, 1))


def dot(a, b, ca=1, cb=0, precision=None):
    return lax.dot_general(
        a, b, (((ca,), (cb,)), ((), ())), precision=precision, preferred_element_type=f32
    )


def iota(shape, axis):
    return lax.broadcasted_iota(jnp.int32, shape, axis)


def sigmoid(z):
    return 0.5 + 0.5 * jnp.tanh(0.5 * z)


def softplus(z):
    return jnp.maximum(z, 0.0) + jnp.log1p(jnp.exp(-jnp.abs(z)))


def segment(starts_ref, n, places):
    found = jnp.full(places.shape, -1, jnp.int32)
    for j in range(starts_ref.shape[1]):
        found = found + (places >= starts_ref[n, j]).astype(jnp.int32)
    return found


def low_half():
    return iota((1, LANES), 1) < LANES // 2


def pair_lanes(cols, j):
    return jnp.where(low_half(), cols[:, 2 * j : 2 * j + 1], cols[:, 2 * j + 1 : 2 * j + 2])


def expand(cols, pairs):
    return jnp.concatenate([pair_lanes(cols, j) for j in range(pairs)], axis=1)


def head_sum(wide):
    rows = wide.shape[1]
    half = LANES // 2
    pick = (iota((rows, LANES), 0) // half == iota((rows, LANES), 1)).astype(f32)
    return dot(wide, pick, precision=highest)


def lower_triangle(q):
    return iota((q, q), 0) >= iota((q, q), 1)


def conv_group(raw_ref, cw_ref, seg, c, q, g):
    lanes = slice(g * LANES, (g + 1) * LANES)
    window = raw_ref[0, c * q : c * q + q + HALO, lanes].astype(f32)
    taps = cw_ref[:, lanes]
    out = taps[4:5] + taps[3:4] * window[HALO:]
    for k in range(1, 4):
        near = seg[HALO:] == seg[HALO - k : HALO - k + q]
        out = out + taps[3 - k : 4 - k] * jnp.where(near, window[HALO - k : HALO - k + q], 0.0)
    return out


def chunk_segments(starts_ref, base_ref, n, c, q):
    first = base_ref[0] + c * q
    cols = segment(starts_ref, n, first - HALO + iota((q + HALO, LANES), 0))
    rows = segment(starts_ref, n, first + iota((8, q), 1))
    return cols, rows


def scan_forward(
    starts_ref,
    base_ref,
    raw_ref,
    cw_ref,
    hp_ref,
    skip_ref,
    act_ref,
    y_ref,
    ent_ref,
    step_ref,
    cum_ref,
    cumr_ref,
    state_ref,
    decay_ref,
    *,
    heads,
    q,
):
    n = pl.program_id(0)
    length = y_ref.shape[1]
    pairs = heads // 2
    wide = pairs * LANES
    tri = lower_triangle(q)
    tri_f = tri.astype(f32)
    state = None
    block = None
    for c in range(length // q):
        rows = slice(c * q, (c + 1) * q)
        seg, seg_r = chunk_segments(starts_ref, base_ref, n, c, q)
        own = seg[HALO:]
        prev = seg[HALO - 1 : HALO]
        act = []
        for g in range(pairs + 2):
            z = conv_group(raw_ref, cw_ref, seg, c, q, g)
            a = z * sigmoid(z)
            act_ref[0, rows, g * LANES : (g + 1) * LANES] = a.astype(bf16)
            act.append(a)
        b_low, c_low = act[pairs].astype(bf16), act[pairs + 1].astype(bf16)
        dt_raw = raw_ref[0, HALO + c * q : HALO + (c + 1) * q, wide + 2 * LANES :].astype(f32)
        used = iota((1, LANES), 1) < heads
        step = jnp.where(used, softplus(dt_raw + hp_ref[0:1]), 0.0)
        cum = dot(tri_f, hp_ref[1:2] * step, precision=highest)
        cum_r = cum.T
        step_ref[0, rows] = step
        cum_ref[0, rows] = cum
        cumr_ref[0, :, rows] = cum_r[:8]
        same = tri & (own[:, :1] == seg_r[:1])
        scores = dot(c_low, b_low, 1, 1)
        last = cum[q - 1 : q]
        ent = jnp.where(own == prev, jnp.exp(cum), 0.0)
        tail = jnp.where(own == own[q - 1 : q], jnp.exp(last - cum), 0.0) * step
        decay = jnp.where(own[q - 1 : q] == prev, jnp.exp(last), 0.0)
        if c:
            state_low = state.astype(bf16)
        new_state = []
        for j in range(pairs):
            lanes = slice(j * LANES, (j + 1) * LANES)
            scaled = act[j] * pair_lanes(step, j)
            out = skip_ref[0:1, lanes] * act[j]
            for half in range(2):
                h = 2 * j + half
                mixing = jnp.exp(jnp.where(same, cum[:, h : h + 1] - cum_r[h : h + 1], MASKED)) * scores
                part = jnp.where(low_half() == (half == 0), scaled, 0.0)
                out = out + dot(mixing.astype(bf16), part.astype(bf16))
            if c:
                out = out + pair_lanes(ent, j) * dot(c_low, state_low[:, lanes])
            y_ref[0, rows, lanes] = out.astype(bf16)
            weighted = (act[j] * pair_lanes(tail, j)).astype(bf16)
            new_state.append(dot(b_low, weighted, 0, 0))
        gained = jnp.concatenate(new_state, axis=1)
        if c:
            ent = ent * block
            block = block * decay
            state = expand(decay, pairs) * state + gained
        else:
            block = decay
            state = gained
        ent_ref[0, rows] = ent
    state_ref[0] = state
    decay_ref[0] = jnp.broadcast_to(expand(block, pairs), (8, wide))


def norm_rows(place_ref, halo_ref, gain_ref, *refs, low, slots):
    out_ref = refs[-1]
    n = pl.program_id(0)
    count = refs[0].shape[0]

    def scaled(rows):
        rows = rows.astype(f32)
        mean = jnp.mean(rows * rows, axis=-1, keepdims=True)
        return (rows * lax.rsqrt(mean + epsilon) * gain_ref[0:1]).astype(bf16)

    out_ref[0, :HALO] = scaled(halo_ref[0])
    for slot in range(slots):
        for k in range(low):

            @pl.when(n == slot)
            def _():
                first = HALO + (k ^ place_ref[0]) * count
                at = pl.ds(pl.multiple_of(first, HALO), count)
                out_ref[0, at] = scaled(refs[low * slot + k][...])


def pick_half(n, refs, split):
    if len(refs) == 1:
        return refs[0][0]
    return jnp.where(n < split, refs[0][0], refs[1][0])


def gate_rows(p, q):
    return pl.ds(pl.multiple_of(HALO + p * q, HALO), q)


def gate_forward(
    place_ref, y_ref, ent_ref, act_ref, enter_ref, gate_ref, gain_ref, *refs, heads, q, split
):
    u_refs, (out_ref, stat_ref, low_ref) = refs[:-3], refs[-3:]
    n, p = pl.program_id(0), pl.program_id(1)
    u_all = pick_half(n, u_refs, split)
    pairs = heads // 2
    wide = pairs * LANES
    ent = ent_ref[0]
    c_low = act_ref[0, :, wide + LANES : wide + 2 * LANES]
    squares = jnp.zeros((q, LANES), f32)
    products = jnp.zeros((q, LANES), f32)
    for j in range(pairs):
        lanes = slice(j * LANES, (j + 1) * LANES)
        y = y_ref[0, :, lanes] + pair_lanes(ent, j) * dot(c_low, enter_ref[0, :, lanes])
        out_ref[0, :, lanes] = y.astype(bf16)
        z = gate_ref[0, gate_rows(p, q), lanes].astype(f32)
        gated = y * (z * sigmoid(z))
        squares = squares + gated * gated
        gated = gated * gain_ref[0:1, lanes]
        low_ref[0, :, lanes] = gated.astype(bf16)
        products = products + gated * u_all[:, lanes].astype(f32)
    squares = jnp.sum(squares, axis=1, keepdims=True)
    products = jnp.sum(products, axis=1, keepdims=True)
    lane = iota((q, LANES), 1)
    packed = jnp.where(lane == 0, squares, jnp.where(lane == 1, products, 0.0))
    stat_ref[0] = packed.T[:8]


def gate_backward(
    place_ref,
    y_ref,
    ent_ref,
    act_ref,
    gate_ref,
    gain_ref,
    stat_ref,
    *refs,
    heads,
    q,
    columns,
    split,
):
    u_refs, (dy_ref, dgate_ref, low_ref, enter_grad_ref, sums_ref) = refs[:-5], refs[-5:]
    n, p = pl.program_id(0), pl.program_id(1)
    u_all = pick_half(n, u_refs, split)
    pairs = heads // 2
    wide = pairs * LANES

    @pl.when(p == 0)
    def _():
        dgate_ref[0, :HALO] = jnp.zeros((HALO, wide), bf16)
        sums_ref[0] = jnp.zeros((8, wide), f32)
        enter_grad_ref[0] = jnp.zeros(enter_grad_ref.shape[1:], f32)

    sums = jnp.concatenate([stat_ref[0], jnp.zeros((LANES - 8, q), f32)], axis=0).T
    scale = lax.rsqrt(sums[:, 0:1] / columns + epsilon)
    pull = scale * scale * scale * sums[:, 1:2] / columns
    ent = ent_ref[0]
    c_low = act_ref[0, :, wide + LANES : wide + 2 * LANES]
    for j in range(pairs):
        lanes = slice(j * LANES, (j + 1) * LANES)
        y = y_ref[0, :, lanes].astype(f32)
        z = gate_ref[0, gate_rows(p, q), lanes].astype(f32)
        u = u_all[:, lanes].astype(f32)
        gain = gain_ref[0:1, lanes]
        sg = sigmoid(z)
        silu = z * sg
        gated = y * silu
        unit = gated * scale
        dgated = scale * gain * u - pull * gated
        dy = dgated * silu
        dy_ref[0, :, lanes] = dy.astype(bf16)
        dgate_ref[0, gate_rows(p, q), lanes] = (
            dgated * y * (sg * (1.0 + z * (1.0 - sg)))
        ).astype(bf16)
        low_ref[0, :, lanes] = (unit * gain).astype(bf16)
        sums_ref[0, 0:1, lanes] += jnp.sum(u * unit, axis=0, keepdims=True)
        sums_ref[0, 1:2, lanes] += jnp.sum(
            dy * act_ref[0, :, lanes].astype(f32), axis=0, keepdims=True
        )
        enter_grad_ref[0, :, lanes] += dot(c_low, (dy * pair_lanes(ent, j)).astype(bf16), 0, 0)


def normed_backward(place_ref, draw_ref, dgate_ref, back_ref, conv_ref, gate_ref, out_ref, *, q):
    p = pl.program_id(1)
    rows = gate_rows(p, q)
    out = dot(draw_ref[0, rows], conv_ref[...], 1, 1) + dot(dgate_ref[0, rows], gate_ref[...], 1, 1)
    out_ref[0] = out.astype(bf16)

    @pl.when(p == pl.num_programs(1) - 1)
    def _():
        out_ref[0, q - HALO :] = (out[q - HALO :] + back_ref[0].astype(f32)).astype(bf16)


def scan_backward_inner(
    starts_ref,
    base_ref,
    act_ref,
    dy_ref,
    step_ref,
    cum_ref,
    cumr_ref,
    dscaled_ref,
    dbc_ref,
    dcum_ref,
    *,
    heads,
    q,
):
    n = pl.program_id(0)
    pairs = heads // 2
    wide = pairs * LANES
    tri = lower_triangle(q)
    for c in range(dy_ref.shape[1] // q):
        rows = slice(c * q, (c + 1) * q)
        first = base_ref[0] + c * q
        seg = segment(starts_ref, n, first + iota((q, LANES), 0))
        seg_r = segment(starts_ref, n, first + iota((8, q), 1))
        same = tri & (seg[:, :1] == seg_r[:1])
        b_low = act_ref[0, rows, wide : wide + LANES]
        c_low = act_ref[0, rows, wide + LANES : wide + 2 * LANES]
        scores = dot(c_low, b_low, 1, 1)
        step = step_ref[0, rows]
        cum = cum_ref[0, rows]
        cum_r = cumr_ref[0, :, rows]
        dscores = jnp.zeros((q, q), f32)
        lane = iota((q, LANES), 1)
        gain_t = jnp.zeros((q, LANES), f32)
        lost = []
        for j in range(pairs):
            lanes = slice(j * LANES, (j + 1) * LANES)
            scaled = (act_ref[0, rows, lanes].astype(f32) * pair_lanes(step, j)).astype(bf16)
            dy = dy_ref[0, rows, lanes].astype(f32)
            out = jnp.zeros((q, LANES), f32)
            for half in range(2):
                h = 2 * j + half
                decays = jnp.exp(jnp.where(same, cum[:, h : h + 1] - cum_r[h : h + 1], MASKED))
                mixing = decays * scores
                part = jnp.where(low_half() == (half == 0), dy, 0.0).astype(bf16)
                dmix = dot(part, scaled, 1, 1) * decays
                dscores = dscores + dmix
                flow = dmix * scores
                gain_t = jnp.where(lane == h, jnp.sum(flow, axis=1, keepdims=True), gain_t)
                lost.append(jnp.sum(flow, axis=0, keepdims=True))
                out = out + dot(mixing.astype(bf16), part, 0, 0)
            dscaled_ref[0, rows, lanes] = out.astype(bf16)
        lost = jnp.concatenate(lost + [jnp.zeros((LANES - heads, q), f32)], axis=0)
        dcum_ref[0, rows] = gain_t - lost.T
        dlow = dscores.astype(bf16)
        dbc_ref[0, rows, :LANES] = dot(dlow, c_low, 0, 0).astype(bf16)
        dbc_ref[0, rows, LANES:] = dot(dlow, b_low).astype(bf16)


def scan_backward_outer(
    starts_ref,
    base_ref,
    raw_ref,
    act_ref,
    dy_ref,
    step_ref,
    cum_ref,
    dscaled_ref,
    dbc_ref,
    dcum_ref,
    enter_ref,
    leave_ref,
    cw_ref,
    hp_ref,
    skip_ref,
    draw_ref,
    dconv_ref,
    dhead_ref,
    dz_ref,
    *,
    heads,
    q,
):
    n = pl.program_id(0)
    length = dy_ref.shape[1]
    chunks = length // q
    pairs = heads // 2
    wide = pairs * LANES
    tri_f = lower_triangle(q).astype(f32)
    used = iota((1, LANES), 1) < heads
    groups = pairs + 2

    prepared = []
    state = enter_ref[0].astype(f32)
    for c in range(chunks):
        rows = slice(c * q, (c + 1) * q)
        seg, _ = chunk_segments(starts_ref, base_ref, n, c, q)
        own, prev = seg[HALO:], seg[HALO - 1 : HALO]
        cum = cum_ref[0, rows]
        last = cum[q - 1 : q]
        ent = jnp.where(own == prev, jnp.exp(cum), 0.0)
        fade = jnp.where(own == own[q - 1 : q], jnp.exp(last - cum), 0.0)
        decay = jnp.where(own[q - 1 : q] == prev, jnp.exp(last), 0.0)
        prepared.append((seg, ent, fade, decay, state))
        if c + 1 < chunks:
            tail = fade * step_ref[0, rows]
            b_low = act_ref[0, rows, wide : wide + LANES]
            gained = [
                dot(
                    b_low,
                    (
                        act_ref[0, rows, j * LANES : (j + 1) * LANES].astype(f32)
                        * pair_lanes(tail, j)
                    ).astype(bf16),
                    0,
                    0,
                )
                for j in range(pairs)
            ]
            state = expand(decay, pairs) * state + jnp.concatenate(gained, axis=1)

    dconv_ref[0] = jnp.zeros(dconv_ref.shape[1:], f32)
    dhead_ref[0] = jnp.zeros(dhead_ref.shape[1:], f32)
    dz_ref[:HALO] = jnp.zeros((HALO, groups * LANES), f32)
    dz_ref[HALO + length :] = jnp.zeros((8, groups * LANES), f32)
    draw_ref[0, :HALO, groups * LANES :] = jnp.zeros((HALO, LANES), bf16)
    grad = leave_ref[0].astype(f32)
    for c in reversed(range(chunks)):
        rows = slice(c * q, (c + 1) * q)
        seg, ent, fade, decay, state = prepared[c]
        step = step_ref[0, rows]
        tail = fade * step
        b_low = act_ref[0, rows, wide : wide + LANES]
        c_low = act_ref[0, rows, wide + LANES : wide + 2 * LANES]
        state_low = state.astype(bf16)
        grad_low = grad.astype(bf16)
        db = dbc_ref[0, rows, :LANES].astype(f32)
        dc = dbc_ref[0, rows, LANES:].astype(f32)
        dx = []
        by_step, by_tail, by_ent, next_grad = [], [], [], []
        for j in range(pairs):
            lanes = slice(j * LANES, (j + 1) * LANES)
            x = act_ref[0, rows, lanes].astype(f32)
            dy = dy_ref[0, rows, lanes].astype(f32)
            dscaled = dscaled_ref[0, rows, lanes].astype(f32)
            dweighted = dot(b_low, grad_low[:, lanes])
            wide_tail = pair_lanes(tail, j)
            entered = (dy * pair_lanes(ent, j)).astype(bf16)
            dx.append(
                dscaled * pair_lanes(step, j) + skip_ref[0:1, lanes] * dy + dweighted * wide_tail
            )
            by_step.append(dscaled * x)
            by_tail.append(dweighted * x)
            by_ent.append(dy * dot(c_low, state_low[:, lanes]))
            db = db + dot((x * wide_tail).astype(bf16), grad_low[:, lanes], 1, 1)
            dc = dc + dot(entered, state_low[:, lanes], 1, 1)
            next_grad.append(dot(c_low, entered, 0, 0))
        dtail = head_sum(jnp.concatenate(by_tail, axis=1))
        dent = head_sum(jnp.concatenate(by_ent, axis=1))
        moved = dtail * tail
        ddecay = head_sum(jnp.sum(grad * state, axis=0, keepdims=True))
        at_last = jnp.sum(moved, axis=0, keepdims=True) + ddecay * decay
        dcum = dcum_ref[0, rows] + dent * ent - moved
        dcum = dcum + jnp.where(iota((q, LANES), 0) == q - 1, at_last, 0.0)
        drates = dot(tri_f, dcum, 0, 0, precision=highest)
        rate = hp_ref[1:2]
        dstep = head_sum(jnp.concatenate(by_step, axis=1)) + dtail * fade + drates * rate
        dt_raw = raw_ref[0, HALO + c * q : HALO + (c + 1) * q, groups * LANES :].astype(f32)
        ddt = jnp.where(used, dstep * sigmoid(dt_raw + hp_ref[0:1]), 0.0)
        draw_ref[0, HALO + c * q : HALO + (c + 1) * q, groups * LANES :] = ddt.astype(bf16)
        dhead_ref[0, 0:1] += jnp.sum(ddt, axis=0, keepdims=True)
        dhead_ref[0, 1:2] += jnp.sum(
            jnp.where(used, drates * (rate * step), 0.0), axis=0, keepdims=True
        )
        grad = expand(decay, pairs) * grad + jnp.concatenate(next_grad, axis=1)
        for g in range(groups):
            lanes = slice(g * LANES, (g + 1) * LANES)
            z = conv_group(raw_ref, cw_ref, seg, c, q, g)
            sg = sigmoid(z)
            dact = dx[g] if g < pairs else (db, dc)[g - pairs]
            dz = dact * (sg * (1.0 + z * (1.0 - sg)))
            dz_ref[HALO + c * q : HALO + (c + 1) * q, lanes] = dz
            window = raw_ref[0, c * q : c * q + q + HALO, lanes].astype(f32)
            dconv_ref[0, 4:5, lanes] += jnp.sum(dz, axis=0, keepdims=True)
            dconv_ref[0, 3:4, lanes] += jnp.sum(dz * window[HALO:], axis=0, keepdims=True)
            for k in range(1, 4):
                near = seg[HALO:] == seg[HALO - k : HALO - k + q]
                source = jnp.where(near, window[HALO - k : HALO - k + q], 0.0)
                dconv_ref[0, 3 - k : 4 - k, lanes] += jnp.sum(dz * source, axis=0, keepdims=True)

    places = base_ref[0] - HALO + iota((HALO + length + 8, LANES), 0)
    seg = segment(starts_ref, n, places)
    total = HALO + length
    for g in range(groups):
        lanes = slice(g * LANES, (g + 1) * LANES)
        taps = cw_ref[:, lanes]
        out = taps[3:4] * dz_ref[:total, lanes]
        for k in range(1, 4):
            near = seg[k : k + total] == seg[:total]
            out = out + taps[3 - k : 4 - k] * jnp.where(near, dz_ref[k : k + total, lanes], 0.0)
        draw_ref[0, :, lanes] = out.astype(bf16)


def per_sequence(shape):
    return pl.BlockSpec((1,) + shape[1:], lambda n, *_: (n, 0, 0))


def shared(shape):
    return pl.BlockSpec(shape, lambda n, *_: (0, 0))


def call(kernel, scalars, inputs, outputs, flops, scratch=(), grid=None, ins=None, outs=None):
    specs = [shared(a.shape) if a.ndim == 2 else per_sequence(a.shape) for a in inputs]
    moved = sum(a.size * a.dtype.itemsize for a in list(inputs) + list(outputs))
    return pl.pallas_call(
        kernel,
        out_shape=outputs,
        grid_spec=pltpu.PrefetchScalarGridSpec(
            num_scalar_prefetch=len(scalars),
            grid=grid or (outputs[0].shape[0],),
            in_specs=ins or specs,
            out_specs=outs or [per_sequence(o.shape) for o in outputs],
            scratch_shapes=list(scratch),
        ),
        cost_estimate=pl.CostEstimate(flops=flops, transcendentals=0, bytes_accessed=moved),
        interpret=INTERPRET,
    )(*scalars, *inputs)


def spread(*shape, dtype=f32):
    return jax.ShapeDtypeStruct(shape, dtype)


def after(value, *others):
    return lax.optimization_barrier((value,) + others)[0]


def is_small():
    return lax.axis_size("lo") == 2 and lax.axis_size("bx") == 2


def gather_pieces(rows, hold):
    if not is_small():
        return [lax.all_gather(rows, PLANE, axis=0, tiled=False)]
    across = lax.ppermute(rows, "bx", SWAP)
    beside = lax.ppermute(rows, "lo", SWAP)
    corner = lax.ppermute(rows, ("lo", "bx"), CROSS)
    half = jnp.stack([after(rows, hold), beside, across, corner])
    return [half, lax.ppermute(half, "core", SWAP)]


def gather_single(rows):
    if not is_small():
        got = lax.all_gather(rows, PLANE, axis=0, tiled=False)
        return [got[i] for i in range(got.shape[0])]
    near = [
        rows,
        lax.ppermute(rows, "lo", SWAP),
        lax.ppermute(rows, "bx", SWAP),
        lax.ppermute(rows, ("lo", "bx"), CROSS),
    ]
    return near + [lax.ppermute(near[i], "core", SWAP) for i in range(4)]


def gather_edges(pieces, rows):
    low = lax.axis_size("lo")
    high = lax.axis_size("hi")
    place = lax.axis_index("lo")
    used = len(pieces) // 2 if is_small() else len(pieces)
    edges = []
    for i in range(0, used, low):
        at = [pieces[i + k][-rows:] for k in range(low)]
        edge = at[0]
        if low == 2:
            edge = jnp.where(place == 1, at[0], at[1])
        edges.append(edge)
    route = tuple((i, i + 1) for i in range(high - 1))
    came = lax.ppermute(jnp.stack(edges), "hi", route)
    if is_small():
        came = jnp.concatenate([came, lax.ppermute(came, "core", SWAP)])
    return came


def scatter_pieces(make):
    if not is_small():
        sent = make(0, lax.axis_size("bx") * lax.axis_size("core"))
        return lax.psum_scatter(sent, PLANE, scatter_dimension=0, tiled=False).astype(f32)
    other = make(2, 2)
    came = lax.ppermute(other, "core", SWAP)
    own = make(0, 2)

    def piece(i):
        return own[i].astype(f32) + came[i].astype(f32)

    beside = lax.ppermute(piece(1).astype(bf16), "lo", SWAP)
    across = lax.ppermute(piece(2).astype(bf16), "bx", SWAP)
    corner = lax.ppermute(piece(3).astype(bf16), ("lo", "bx"), CROSS)
    return piece(0) + across.astype(f32) + beside.astype(f32) + corner.astype(f32)


def sum_plane(stats):
    if not is_small():
        return lax.psum(stats, PLANE)
    rest = stats.shape[1:]
    grid = stats.reshape((2, 2) + rest)
    grid = grid + lax.ppermute(grid[::-1], "core", SWAP)
    grid = grid + lax.ppermute(grid[:, ::-1], "bx", SWAP)
    grid = grid + lax.ppermute(grid, "lo", SWAP)
    return grid.reshape(stats.shape)


def gather_starts(starts):
    if not is_small():
        return lax.all_gather(starts, ("bx", "core"), axis=0, tiled=True)
    half = jnp.concatenate([starts, lax.ppermute(starts, "bx", SWAP)])
    return jnp.concatenate([half, lax.ppermute(half, "core", SWAP)])


def piece_of(low, offset=0):
    def index(n, p, place):
        return (low * n + (p ^ place[0]) - offset, 0, 0)

    return index


def half_specs(halves, shape, low):
    count = halves[0].shape[0]
    specs = []
    for h in range(len(halves)):

        def index(n, p, place, h=h):
            return (jnp.clip(low * n + (p ^ place[0]) - h * count, 0, count - 1), 0, 0)

        specs.append(pl.BlockSpec((1,) + shape, index))
    return specs


def chain(state, decay, forward):
    size = lax.axis_size("hi")
    place = lax.axis_index("hi")
    enter = jnp.zeros(state.shape, bf16)
    for k in range(size - 1):
        source = k if forward else size - 1 - k
        target = source + 1 if forward else source - 1
        passed = (state + decay * enter.astype(f32)).astype(bf16)
        came = lax.ppermute(passed, "hi", ((source, target),))
        enter = jnp.where(place == target, came, enter)
    return enter


def to_shards(columns, width):
    low = lax.axis_size("lo")
    batch = lax.axis_size("bx") * lax.axis_size("core")
    rows = columns.shape[0]
    split = columns.reshape(rows, batch, low, width)
    return jnp.transpose(split, (2, 1, 0, 3)).reshape(low * batch, rows, width)


def from_shards(blocks):
    low = lax.axis_size("lo")
    batch = lax.axis_size("bx") * lax.axis_size("core")
    _, rows, width = blocks.shape
    split = blocks.reshape(low, batch, rows, width)
    return jnp.transpose(split, (2, 1, 0, 3)).reshape(rows, batch * low * width)


def exchange(blocks, axes=PLANE):
    return lax.all_to_all(blocks, axes, 0, 0, tiled=True)


def step_of(
    residual_in,
    seg_ids,
    doc_starts,
    norm_gain,
    in_weight,
    conv_weight,
    conv_bias,
    dt_bias,
    a_log,
    skip_weight,
    gate_gain,
    out_weight,
    cotangent,
):
    high, low = lax.axis_size("hi"), lax.axis_size("lo")
    batch = lax.axis_size("bx") * lax.axis_size("core")
    team = low * batch
    devices = high * team
    row_count, features = residual_in.shape[1:]
    heads = dt_bias.shape[0] // team
    inner = gate_gain.shape[0] * devices
    channels = conv_bias.shape[0] * devices
    width = inner // team
    shared_width = channels - inner
    taps = conv_weight.shape[1]
    length = low * row_count
    q = row_count
    total = HALO + length
    pad_width = width + shared_width + LANES
    at_dt = width + shared_width
    k_rows = in_weight.shape[0]
    o_rows = out_weight.shape[0]
    sequences = batch
    place_low = lax.axis_index("lo")
    place_batch = lax.axis_index("bx") * lax.axis_size("core") + lax.axis_index("core")
    shard = place_batch * low + place_low
    place = place_low.reshape(1).astype(jnp.int32)
    base = (lax.axis_index("hi") * length).reshape(1).astype(jnp.int32)

    lanes_of = conv_bias.shape[0]
    small = jnp.stack(
        [conv_weight[:, k] for k in range(taps)]
        + [conv_bias]
        + [jnp.pad(gain, (0, lanes_of - gain.shape[0])) for gain in (gate_gain, norm_gain)]
    )
    small = jnp.pad(small, ((0, 8 - taps - 3), (0, LANES - lanes_of))).reshape(-1)
    small_lanes = -(-small.shape[0] // k_rows)
    small = jnp.pad(small, (0, small_lanes * k_rows - 8 * LANES)).reshape(k_rows, small_lanes)
    at_small = at_dt + heads
    block = jnp.concatenate(
        [
            to_shards(in_weight[:, inner : 2 * inner], width),
            jnp.broadcast_to(
                in_weight[:, 2 * inner : inner + channels], (team, k_rows, shared_width)
            ),
            to_shards(in_weight[:, inner + channels :], heads),
            jnp.broadcast_to(small, (team, k_rows, small_lanes)),
            jnp.zeros((team, k_rows, pad_width - at_small - small_lanes), bf16),
        ],
        axis=2,
    )
    rows_of_plane = exchange(block)
    small = rows_of_plane[:, :, at_small : at_small + small_lanes].reshape(team, -1)
    small = small[:, : 8 * LANES].reshape(team, 8, LANES)
    rows_of_plane = rows_of_plane.reshape(team * k_rows, pad_width)
    conv_w = lax.all_gather(rows_of_plane, "hi", axis=0, tiled=True)

    resid = gather_single(after(residual_in[0], rows_of_plane))
    starts = gather_starts(after(doc_starts, rows_of_plane))
    halo = gather_edges(resid, HALO)

    small = lax.all_gather(small, "hi", axis=0, tiled=False).reshape(devices, 8, LANES)
    small = jnp.swapaxes(small.astype(f32), 0, 1)
    table = small[: taps + 1, :, :lanes_of].reshape(taps + 1, channels)
    full_gate = small[taps + 1, :, : gate_gain.shape[0]].reshape(1, inner)
    full_gain = small[taps + 2, :, : norm_gain.shape[0]].reshape(1, features)
    cw = jnp.concatenate(
        [lax.dynamic_slice_in_dim(table, shard * width, width, 1), table[:, inner:]], axis=1
    )
    cw = jnp.pad(cw, ((0, 8 - taps - 1), (0, 0)))
    gain_row = jnp.broadcast_to(
        lax.dynamic_slice_in_dim(full_gate, shard * width, width, 1), (8, width)
    )
    own_head = functools.partial(
        lax.dynamic_slice_in_dim, start_index=shard * heads, slice_size=heads
    )
    hp = jnp.stack([own_head(dt_bias), -jnp.exp(own_head(a_log))])
    hp = jnp.pad(hp, ((0, 6), (0, LANES - heads)))
    skip_row = jnp.broadcast_to(jnp.repeat(own_head(skip_weight), width // heads), (8, width))

    sub = features // width
    gate_block = exchange(after(to_shards(in_weight[:, :inner], width), rows_of_plane))
    gate_block = gate_block.reshape(sub, -1, width)
    gate_block = jnp.concatenate([gate_block[i] for i in range(sub)], axis=1)
    gate_rows_count = gate_block.shape[0]
    second = lax.all_gather(
        jnp.concatenate([gate_block, out_weight]), "hi", axis=0, tiled=False
    )

    norm_row = jnp.broadcast_to(full_gain, (8, features))
    (normed,) = call(
        functools.partial(norm_rows, low=low, slots=sequences),
        (place,),
        [halo, norm_row] + resid,
        (spread(sequences, total, features, dtype=bf16),),
        sequences * total * features * 10,
    )
    flat = normed.reshape(-1, features)
    raw = dot(flat, conv_w).astype(bf16).reshape(sequences, total, pad_width)

    act_shape = (sequences, length, width + shared_width)
    wide_shape = (sequences, length, width)
    col_shape = (sequences, length, LANES)
    row_shape = (sequences, 8, length)
    state_shape = (sequences, shared_width // 2, width)
    unit = sequences * length * width
    act, y_local, ent, step, cum, cum_r, state, decay = call(
        functools.partial(scan_forward, heads=heads, q=q),
        (starts, base),
        (raw, cw, hp, skip_row),
        (
            spread(*act_shape, dtype=bf16),
            spread(*wide_shape, dtype=bf16),
            spread(*col_shape),
            spread(*col_shape),
            spread(*col_shape),
            spread(*row_shape),
            spread(*state_shape),
            spread(sequences, 8, width),
        ),
        unit * 8 * q,
    )
    cot = gather_pieces(after(cotangent[0], normed), state)
    split = sequences // len(cot)
    decay = decay[:, :1]
    enter = chain(state, decay, True)

    gate_w = jnp.concatenate(
        [
            second[:, None, :gate_rows_count, i * width : (i + 1) * width]
            for i in range(sub)
        ],
        axis=1,
    ).reshape(features, width)
    gate = dot(flat, gate_w).astype(bf16).reshape(sequences, total, width)
    out_w = second[:, gate_rows_count:]
    out_w = exchange(out_w, ("bx", "core")).reshape(batch, high // batch, o_rows, features)
    out_w = jnp.swapaxes(out_w, 0, 1).reshape(width, features)
    u = [
        dot(half.reshape(-1, features), out_w, 1, 1).astype(bf16).reshape(-1, row_count, width)
        for half in cot
    ]

    def chunk(lanes):
        return pl.BlockSpec((1, q, lanes), lambda n, p, place: (n, p, 0))

    def whole(rows, lanes):
        return pl.BlockSpec((1, rows, lanes), lambda n, p, place: (n, 0, 0))

    def fixed(a):
        return pl.BlockSpec(a.shape, lambda n, p, place: (0, 0))

    across = pl.BlockSpec((1, 8, q), lambda n, p, place: (n, 0, p))
    states = whole(*state_shape[1:])
    u_specs = half_specs(cot, (row_count, width), low)
    grid = (sequences, low)
    y, stats, unscaled = call(
        functools.partial(gate_forward, heads=heads, q=q, split=split),
        (place,),
        [y_local, ent, act, enter, gate, gain_row] + u,
        (
            spread(*wide_shape, dtype=bf16),
            spread(*row_shape),
            spread(team, row_count, width, dtype=bf16),
        ),
        unit * 300,
        grid=grid,
        ins=[
            chunk(width),
            chunk(LANES),
            chunk(width + shared_width),
            states,
            whole(total, width),
            fixed(gain_row),
        ]
        + u_specs,
        outs=[chunk(width), across, pl.BlockSpec((1, q, width), piece_of(low))],
    )
    stats = sum_plane(stats)
    my_slot = 0 if is_small() else place_batch

    def mixed_pieces(first, slots):
        rows = unscaled[first * low : (first + slots) * low].reshape(-1, width)
        return dot(rows, out_w).astype(bf16).reshape(-1, row_count, features)

    mixed = scatter_pieces(mixed_pieces)
    own_squares = lax.dynamic_slice_in_dim(stats[my_slot, 0], place_low * row_count, row_count)
    mixed_scale = lax.rsqrt(own_squares / inner + epsilon)[:, None]
    mixed_out = (residual_in[0].astype(f32) + mixed_scale * mixed).astype(bf16)

    dy, dgate, mixer_low, enter_grad, gate_sums = call(
        functools.partial(gate_backward, heads=heads, q=q, columns=inner, split=split),
        (place,),
        [y, ent, act, gate, gain_row, stats] + u,
        (
            spread(*wide_shape, dtype=bf16),
            spread(sequences, total, width, dtype=bf16),
            spread(team, row_count, width, dtype=bf16),
            spread(*state_shape),
            spread(sequences, 8, width),
        ),
        unit * 300,
        grid=grid,
        ins=[
            chunk(width),
            chunk(LANES),
            chunk(width + shared_width),
            whole(total, width),
            fixed(gain_row),
            across,
        ]
        + u_specs,
        outs=[
            chunk(width),
            whole(total, width),
            pl.BlockSpec((1, q, width), piece_of(low)),
            states,
            whole(8, width),
        ],
    )
    leave = chain(enter_grad, decay, False)
    gate_sums = jnp.sum(gate_sums, axis=0)
    dskip = jnp.sum(gate_sums[1].reshape(heads, -1), axis=1)
    gain_all = lax.dynamic_update_slice(
        jnp.zeros((1, inner), f32), gate_sums[:1], (0, shard * width)
    )

    count = cot[0].shape[0]
    out_grad = 0.0
    for h, half in enumerate(cot):
        rows = mixer_low[h * count : (h + 1) * count].reshape(-1, width)
        out_grad = out_grad + dot(rows, half.reshape(-1, features), 0, 0)
    out_grad = out_grad.astype(bf16).reshape(high // batch, batch, o_rows, features)
    out_grad = exchange(
        jnp.swapaxes(out_grad, 0, 1).reshape(high, o_rows, features), ("bx", "core")
    )
    dgate_flat = dgate.reshape(-1, width)
    gate_grad = dot(flat, dgate_flat, 0, 0).astype(bf16)
    gate_grad = gate_grad.reshape(high, sub, gate_rows_count, width)
    gate_grad = jnp.concatenate([gate_grad[:, i] for i in range(sub)], axis=2)
    early = jnp.concatenate([gate_grad, out_grad], axis=1)
    early = lax.psum_scatter(early, "hi", scatter_dimension=0, tiled=False)

    dscaled, dbc, dcum = call(
        functools.partial(scan_backward_inner, heads=heads, q=q),
        (starts, base),
        (act, dy, step, cum, cum_r),
        (
            spread(*wide_shape, dtype=bf16),
            spread(sequences, length, shared_width, dtype=bf16),
            spread(*col_shape),
        ),
        unit * 16 * q,
    )
    draw, dconv, dhead = call(
        functools.partial(scan_backward_outer, heads=heads, q=q),
        (starts, base),
        (raw, act, dy, step, cum, dscaled, dbc, dcum, enter, leave, cw, hp, skip_row),
        (
            spread(sequences, total, pad_width, dtype=bf16),
            spread(sequences, 8, width + shared_width),
            spread(sequences, 8, LANES),
        ),
        unit * 2000,
        scratch=(pltpu.VMEM((total + 8, width + shared_width), f32),),
    )
    draw_flat = draw.reshape(-1, pad_width)

    edge_rows = draw[:, :HALO].reshape(-1, pad_width)
    returned = lax.ppermute(
        dot(edge_rows, conv_w, 1, 1).astype(bf16).reshape(sequences, HALO, features),
        "hi",
        tuple((i + 1, i) for i in range(high - 1)),
    )

    late = dot(flat, draw_flat, 0, 0).astype(bf16)
    dconv = jnp.sum(dconv, axis=0)
    dhead = jnp.sum(dhead, axis=0)

    def placed(mine, size):
        return lax.dynamic_update_slice(
            jnp.zeros((mine.shape[0], size), f32), mine, (0, shard * mine.shape[1])
        )

    by_owner = jnp.concatenate(
        [placed(dconv[: taps + 1, :width], inner), dconv[: taps + 1, width:]], axis=1
    ).reshape(taps + 1, devices, lanes_of)
    heads_all = placed(jnp.concatenate([dhead[:2, :heads], dskip[None]]), heads * team)
    spare = pad_width - at_dt - heads

    def rows_for_owners(array):
        array = jnp.broadcast_to(array, (array.shape[0], devices, array.shape[2]))
        return jnp.pad(array, ((0, 0), (0, 0), (0, spare - array.shape[2])))

    spare_rows = jnp.concatenate(
        [
            rows_for_owners(by_owner),
            rows_for_owners(gain_all.reshape(1, devices, -1)),
            rows_for_owners(heads_all[:, None]),
        ]
    )
    spare_rows = jnp.swapaxes(spare_rows, 0, 1)
    spare_rows = jnp.pad(spare_rows, ((0, 0), (0, k_rows - spare_rows.shape[1]), (0, 0)))
    spare_rows = spare_rows.reshape(devices * k_rows, spare).astype(bf16)
    late = jnp.concatenate([late[:, : at_dt + heads], spare_rows], axis=1)
    late_sum = lax.psum_scatter(late, "hi", scatter_dimension=0, tiled=True)

    def grad_pieces(first, slots):
        def slot(n, p, place):
            return (n + first, 0, 0)

        (out,) = call(
            functools.partial(normed_backward, q=q),
            (place,),
            (draw, dgate, returned, conv_w, gate_w),
            (spread(slots * low, row_count, features, dtype=bf16),),
            2 * slots * length * features * (pad_width + width),
            grid=(slots, low),
            ins=[
                pl.BlockSpec((1, total, pad_width), slot),
                pl.BlockSpec((1, total, width), slot),
                pl.BlockSpec((1, HALO, features), slot),
                fixed(conv_w),
                fixed(gate_w),
            ],
            outs=[pl.BlockSpec((1, q, features), piece_of(low))],
        )
        return out

    own_grad = scatter_pieces(grad_pieces)
    own_grad = own_grad * full_gain
    own = residual_in[0].astype(f32)
    own_scale = lax.rsqrt(jnp.mean(own * own, axis=-1, keepdims=True) + epsilon)
    unit_rows = own * own_scale
    along = jnp.mean(own_grad * unit_rows, axis=-1, keepdims=True)
    input_grad = cotangent[0].astype(f32) + own_scale * (own_grad - unit_rows * along)

    gate_share = jnp.concatenate(
        [early[None, :gate_rows_count, i * width : (i + 1) * width] for i in range(sub)]
    )
    gate_share = exchange(gate_share.reshape(team, k_rows, width))
    gate_share = from_shards(gate_share).astype(f32)
    out_share = early[gate_rows_count:].astype(f32)
    late_share = exchange(late_sum.reshape(team, k_rows, pad_width)).astype(f32)
    summed = jnp.sum(late_share[:, :, width:], axis=0)
    little = summed[:, shared_width + heads :]
    in_share = jnp.concatenate(
        [
            gate_share,
            from_shards(late_share[:, :, :width]),
            summed[:, :shared_width],
            from_shards(late_share[:, :, at_dt : at_dt + heads]),
        ],
        axis=1,
    )
    norm_share = jnp.sum(in_share * in_weight.astype(f32), axis=1) / norm_gain.astype(f32)
    return (
        mixed_out[None],
        input_grad[None],
        norm_share,
        in_share,
        little[:taps, :lanes_of].T,
        little[taps, :lanes_of],
        little[taps + 2, : heads * team],
        little[taps + 3, : heads * team],
        little[taps + 4, : heads * team],
        little[taps + 1, : gate_gain.shape[0]],
        out_share,
    )


def solution(mesh):
    seq, batch = mesh.shape["seq"], mesh.shape["batch"]
    low = max(1, 8 // batch)
    split = Mesh(
        mesh.devices.reshape(seq // low, low, batch // 2, 2), ("hi", "lo", "bx", "core")
    )
    everything = ("hi", "lo", "bx", "core")
    batches, blocks = ("bx", "core"), ("hi", "lo")
    rows = P(batches, blocks, None)
    return jax.shard_map(
        step_of,
        mesh=split,
        in_specs=(
            rows,
            P(batches, blocks),
            P(batches, None),
            P(everything),
            P(everything, None),
            P(everything, None),
            P(everything),
            P(),
            P(),
            P(),
            P(everything),
            P(everything, None),
            rows,
        ),
        out_specs=(
            rows,
            rows,
            P(everything),
            P(everything, None),
            P(everything, None),
            P(everything),
            P(),
            P(),
            P(),
            P(everything),
            P(everything, None),
        ),
        check_vma=False,
    )
```

```python
import functools

import jax
import jax.numpy as jnp
from jax import lax
from jax.experimental import pallas as pl
from jax.experimental.pallas import tpu as pltpu
from jax.sharding import Mesh, PartitionSpec as P


f32 = jnp.float32
bf16 = jnp.bfloat16
epsilon = 1e-05
HALO = 16
LANES = 128
MASKED = -1e30
INTERPRET = False
PLANE = ("lo", "bx", "core")
SWAP = ((0, 1), (1, 0))
CROSS = ((0, 3), (3, 0), (1, 2), (2, 1))


def dot(a, b, ca=1, cb=0, precision=None):
    return lax.dot_general(
        a, b, (((ca,), (cb,)), ((), ())), precision=precision, preferred_element_type=f32
    )


def iota(shape, axis):
    return lax.broadcasted_iota(jnp.int32, shape, axis)


def sigmoid(z):
    return 0.5 + 0.5 * jnp.tanh(0.5 * z)


def softplus(z):
    return jnp.maximum(z, 0.0) + jnp.log1p(jnp.exp(-jnp.abs(z)))


def segment(starts_ref, n, places):
    found = jnp.full(places.shape, -1, jnp.int32)
    for j in range(starts_ref.shape[1]):
        found = found + (places >= starts_ref[n, j]).astype(jnp.int32)
    return found


def low_half():
    return iota((1, LANES), 1) < LANES // 2


def pair_lanes(cols, j):
    return jnp.where(low_half(), cols[:, 2 * j : 2 * j + 1], cols[:, 2 * j + 1 : 2 * j + 2])


def expand(cols, pairs):
    return jnp.concatenate([pair_lanes(cols, j) for j in range(pairs)], axis=1)


def head_sum(wide):
    rows = wide.shape[1]
    half = LANES // 2
    pick = (iota((rows, LANES), 0) // half == iota((rows, LANES), 1)).astype(bf16)
    return dot(wide.astype(bf16), pick)


def exact_dot(ones, values):
    total = 0.0
    for _ in range(3):
        term = values.astype(bf16)
        total = total + dot(ones, term)
        values = values - term.astype(f32)
    return total


def conv_group(raw_ref, cw_ref, win_ref, near, c, q, g):
    lanes = slice(g * LANES, (g + 1) * LANES)
    win_ref[g] = raw_ref[0, c * q : c * q + q + HALO, lanes].astype(f32)
    taps = cw_ref[:, lanes]
    out = taps[4:5] + taps[3:4] * win_ref[g, HALO : HALO + q]
    for k in range(1, 4):
        shifted = win_ref[g, HALO - k : HALO - k + q]
        out = out + taps[3 - k : 4 - k] * jnp.where(near[k - 1], shifted, 0.0)
    return out


def chunk_segments(starts_ref, base_ref, n, c, q):
    first = base_ref[0] + c * q
    cols = segment(starts_ref, n, first - HALO + iota((q + HALO, LANES), 0))
    rows = segment(starts_ref, n, first + iota((8, q), 1))
    return cols, rows


def scan_forward(
    starts_ref,
    base_ref,
    raw_ref,
    cw_ref,
    hp_ref,
    skip_ref,
    act_ref,
    slope_ref,
    y_ref,
    ent_ref,
    step_ref,
    cum_ref,
    cumr_ref,
    state_ref,
    decay_ref,
    win_ref,
    *,
    heads,
    q,
):
    n = pl.program_id(0)
    length = y_ref.shape[1]
    pairs = heads // 2
    wide = pairs * LANES
    lower = (iota((q, q), 0) >= iota((q, q), 1)).astype(bf16)
    state = None
    block = None
    for c in range(length // q):
        rows = slice(c * q, (c + 1) * q)
        seg, seg_r = chunk_segments(starts_ref, base_ref, n, c, q)
        own = seg[HALO:]
        prev = seg[HALO - 1 : HALO]
        near = [own == seg[HALO - k : HALO - k + q] for k in range(1, 4)]
        act = []
        for g in range(pairs + 2):
            lanes = slice(g * LANES, (g + 1) * LANES)
            z = conv_group(raw_ref, cw_ref, win_ref, near, c, q, g)
            sg = sigmoid(z)
            a = z * sg
            act_ref[0, rows, lanes] = a.astype(bf16)
            slope_ref[0, rows, lanes] = (sg + a * (1.0 - sg)).astype(bf16)
            act.append(a)
        b_low, c_low = act[pairs].astype(bf16), act[pairs + 1].astype(bf16)
        dt_raw = raw_ref[0, HALO + c * q : HALO + (c + 1) * q, wide + 2 * LANES :].astype(f32)
        used = iota((1, LANES), 1) < heads
        step = jnp.where(used, softplus(dt_raw + hp_ref[0:1]), 0.0)
        cum = exact_dot(lower, hp_ref[1:2] * step)
        cum_r = cum.T
        step_ref[0, rows] = step
        cum_ref[0, rows] = cum
        cumr_ref[0, :, rows] = cum_r[:8]
        scores = dot(c_low, b_low, 1, 1)
        parts = []
        for top, end in ((0, q),):
            at = slice(top, end)
            causal = iota((q, end), 0) >= iota((q, end), 1)
            same = causal & (own[at, :1] == seg_r[:1, :end])
            parts.append((at, end, jnp.where(same, 0.0, MASKED)))
        last = cum[q - 1 : q]
        ent = jnp.where(own == prev, jnp.exp(cum), 0.0)
        tail = jnp.where(own == own[q - 1 : q], jnp.exp(last - cum), 0.0) * step
        decay = jnp.where(own[q - 1 : q] == prev, jnp.exp(last), 0.0)
        if c:
            state_low = state.astype(bf16)
        new_state = []
        for j in range(pairs):
            lanes = slice(j * LANES, (j + 1) * LANES)
            scaled = act[j] * pair_lanes(step, j)
            halves = [
                jnp.where(low_half() == (half == 0), scaled, 0.0).astype(bf16) for half in range(2)
            ]
            within = []
            for at, end, bias in parts:
                mixing = []
                for half in range(2):
                    h = 2 * j + half
                    decays = jnp.exp(cum[at, h : h + 1] - cum_r[h : h + 1, :end] + bias)
                    mixing.append((decays * scores[at, :end]).astype(bf16))
                out = dot(jnp.concatenate(mixing, axis=1), jnp.concatenate(halves, axis=0))
                within.append(out)
            out = skip_ref[0:1, lanes] * act[j] + jnp.concatenate(within, axis=0)
            if c:
                out = out + pair_lanes(ent, j) * dot(c_low, state_low[:, lanes])
            y_ref[0, rows, lanes] = out.astype(bf16)
            weighted = (act[j] * pair_lanes(tail, j)).astype(bf16)
            new_state.append(dot(b_low, weighted, 0, 0))
        gained = jnp.concatenate(new_state, axis=1)
        if c:
            ent = ent * block
            block = block * decay
            state = expand(decay, pairs) * state + gained
        else:
            block = decay
            state = gained
        ent_ref[0, rows] = ent
    state_ref[0] = state
    decay_ref[0] = jnp.broadcast_to(expand(block, pairs), (8, wide))


def norm_rows(place_ref, halo_ref, gain_ref, *refs, low, slots):
    out_ref = refs[-1]
    n = pl.program_id(0)
    count = refs[0].shape[0]

    def scaled(rows):
        rows = rows.astype(f32)
        mean = jnp.mean(rows * rows, axis=-1, keepdims=True)
        return (rows * lax.rsqrt(mean + epsilon) * gain_ref[0:1]).astype(bf16)

    out_ref[0, :HALO] = scaled(halo_ref[0])
    for slot in range(slots):
        for k in range(low):

            @pl.when(n == slot)
            def _():
                first = HALO + (k ^ place_ref[0]) * count
                at = pl.ds(pl.multiple_of(first, HALO), count)
                out_ref[0, at] = scaled(refs[low * slot + k][...])


def pick_half(n, refs, split):
    if len(refs) == 1:
        return refs[0][0]
    return jnp.where(n < split, refs[0][0], refs[1][0])


def gate_rows(p, q):
    return pl.ds(pl.multiple_of(HALO + p * q, HALO), q)


def gate_forward(
    place_ref, y_ref, ent_ref, act_ref, enter_ref, gate_ref, gain_ref, *refs, heads, q, split
):
    u_refs, (out_ref, stat_ref, low_ref) = refs[:-3], refs[-3:]
    n, p = pl.program_id(0), pl.program_id(1)
    u_all = pick_half(n, u_refs, split)
    pairs = heads // 2
    wide = pairs * LANES
    ent = ent_ref[0]
    c_low = act_ref[0, :, wide + LANES : wide + 2 * LANES]
    squares = jnp.zeros((q, LANES), f32)
    products = jnp.zeros((q, LANES), f32)
    for j in range(pairs):
        lanes = slice(j * LANES, (j + 1) * LANES)
        y = y_ref[0, :, lanes] + pair_lanes(ent, j) * dot(c_low, enter_ref[0, :, lanes])
        out_ref[0, :, lanes] = y.astype(bf16)
        z = gate_ref[0, gate_rows(p, q), lanes].astype(f32)
        gated = y * (z * sigmoid(z))
        squares = squares + gated * gated
        gated = gated * gain_ref[0:1, lanes]
        low_ref[0, :, lanes] = gated.astype(bf16)
        products = products + gated * u_all[:, lanes].astype(f32)
    squares = jnp.sum(squares, axis=1, keepdims=True)
    products = jnp.sum(products, axis=1, keepdims=True)
    lane = iota((q, LANES), 1)
    packed = jnp.where(lane == 0, squares, jnp.where(lane == 1, products, 0.0))
    stat_ref[0] = packed.T[:8]


def gate_backward(
    place_ref,
    y_ref,
    ent_ref,
    act_ref,
    gate_ref,
    gain_ref,
    stat_ref,
    *refs,
    heads,
    q,
    columns,
    split,
):
    u_refs, (dy_ref, dgate_ref, low_ref, enter_grad_ref, sums_ref) = refs[:-5], refs[-5:]
    n, p = pl.program_id(0), pl.program_id(1)
    u_all = pick_half(n, u_refs, split)
    pairs = heads // 2
    wide = pairs * LANES

    @pl.when(p == 0)
    def _():
        dgate_ref[0, :HALO] = jnp.zeros((HALO, wide), bf16)
        sums_ref[0] = jnp.zeros((8, wide), f32)
        enter_grad_ref[0] = jnp.zeros(enter_grad_ref.shape[1:], f32)

    sums = jnp.concatenate([stat_ref[0], jnp.zeros((LANES - 8, q), f32)], axis=0).T
    scale = lax.rsqrt(sums[:, 0:1] / columns + epsilon)
    pull = scale * scale * scale * sums[:, 1:2] / columns
    ent = ent_ref[0]
    c_low = act_ref[0, :, wide + LANES : wide + 2 * LANES]
    for j in range(pairs):
        lanes = slice(j * LANES, (j + 1) * LANES)
        y = y_ref[0, :, lanes].astype(f32)
        z = gate_ref[0, gate_rows(p, q), lanes].astype(f32)
        u = u_all[:, lanes].astype(f32)
        gain = gain_ref[0:1, lanes]
        sg = sigmoid(z)
        silu = z * sg
        gated = y * silu
        unit = gated * scale
        dgated = scale * gain * u - pull * gated
        dy = dgated * silu
        dy_ref[0, :, lanes] = dy.astype(bf16)
        dgate_ref[0, gate_rows(p, q), lanes] = (
            dgated * y * (sg * (1.0 + z * (1.0 - sg)))
        ).astype(bf16)
        low_ref[0, :, lanes] = (unit * gain).astype(bf16)
        sums_ref[0, 0:1, lanes] += jnp.sum(u * unit, axis=0, keepdims=True)
        sums_ref[0, 1:2, lanes] += jnp.sum(
            dy * act_ref[0, :, lanes].astype(f32), axis=0, keepdims=True
        )
        enter_grad_ref[0, :, lanes] += dot(c_low, (dy * pair_lanes(ent, j)).astype(bf16), 0, 0)


def normed_backward(place_ref, draw_ref, dgate_ref, back_ref, conv_ref, gate_ref, out_ref, *, q):
    p = pl.program_id(1)
    rows = gate_rows(p, q)
    out = dot(draw_ref[0, rows], conv_ref[...], 1, 1) + dot(dgate_ref[0, rows], gate_ref[...], 1, 1)
    out_ref[0] = out.astype(bf16)

    @pl.when(p == pl.num_programs(1) - 1)
    def _():
        out_ref[0, q - HALO :] = (out[q - HALO :] + back_ref[0].astype(f32)).astype(bf16)


def scan_backward_inner(
    starts_ref,
    base_ref,
    act_ref,
    dy_ref,
    step_ref,
    cum_ref,
    cumr_ref,
    dscaled_ref,
    dbc_ref,
    dcum_ref,
    *,
    heads,
    q,
):
    n = pl.program_id(0)
    pairs = heads // 2
    wide = pairs * LANES
    rows = slice(0, q)
    first = base_ref[0] + pl.program_id(1) * q
    seg = segment(starts_ref, n, first + iota((q, LANES), 0))
    seg_r = segment(starts_ref, n, first + iota((8, q), 1))
    b_low = act_ref[0, rows, wide : wide + LANES]
    c_low = act_ref[0, rows, wide + LANES : wide + 2 * LANES]
    scores = dot(b_low, c_low, 1, 1)
    step = step_ref[0, rows]
    cum = cum_ref[0, rows]
    cum_r = cumr_ref[0, :, rows]
    parts = []
    for top in (0,):
        at = slice(top, top + q)
        shape = (q, q - top)
        causal = iota(shape, 0) <= iota(shape, 1)
        same = causal & (seg[at, :1] == seg_r[:1, top:])
        parts.append((at, top, jnp.where(same, 0.0, MASKED)))
    dscores = [jnp.zeros((q, q), f32)]
    lane = iota((q, LANES), 1)
    lost = [jnp.zeros((q, LANES), f32)]
    gains = []
    for j in range(pairs):
        lanes = slice(j * LANES, (j + 1) * LANES)
        scaled = (act_ref[0, rows, lanes].astype(f32) * pair_lanes(step, j)).astype(bf16)
        dy = dy_ref[0, rows, lanes]
        mixing = []
        both = jnp.concatenate(
            [jnp.where(low_half() == (half == 0), dy, jnp.zeros_like(dy)) for half in range(2)],
            axis=0,
        )
        dboth = dot(scaled, both, 1, 1)
        for half in range(2):
            h = 2 * j + half
            gain = []
            for i, (at, top, bias) in enumerate(parts):
                decays = jnp.exp(cum_r[h : h + 1, top:] - cum[at, h : h + 1] + bias)
                dmix = dboth[:, half * q : (half + 1) * q] * decays
                dscores[i] = dscores[i] + dmix
                flow = dmix * scores[at, top:]
                lost[i] = jnp.where(lane == h, jnp.sum(flow, axis=1, keepdims=True), lost[i])
                gain.append(jnp.sum(flow, axis=0, keepdims=True))
                mixing.append((decays * scores[at, top:]).astype(bf16))
            gains.append(gain[0])
        dscaled_ref[0, rows, lanes] = dot(
            jnp.concatenate(mixing, axis=1), both
        ).astype(bf16)
    gains = jnp.concatenate(gains + [jnp.zeros((LANES - heads, q), f32)], axis=0)
    dcum_ref[0, rows] = gains.T - jnp.concatenate(lost, axis=0)
    low = dscores[0].astype(bf16)
    dbc_ref[0, rows, :LANES] = dot(low, c_low).astype(bf16)
    dbc_ref[0, rows, LANES:] = dot(low, b_low, 0, 0).astype(bf16)


def scan_backward_outer(
    starts_ref,
    base_ref,
    raw_ref,
    act_ref,
    slope_ref,
    dy_ref,
    step_ref,
    cum_ref,
    dscaled_ref,
    dbc_ref,
    dcum_ref,
    enter_ref,
    leave_ref,
    cw_ref,
    hp_ref,
    skip_ref,
    draw_ref,
    dconv_ref,
    dhead_ref,
    dz_ref,
    *,
    heads,
    q,
):
    n = pl.program_id(0)
    length = dy_ref.shape[1]
    chunks = length // q
    pairs = heads // 2
    wide = pairs * LANES
    upper = (iota((q, q), 0) <= iota((q, q), 1)).astype(bf16)
    used = iota((1, LANES), 1) < heads
    groups = pairs + 2

    prepared = []
    state = enter_ref[0].astype(f32)
    for c in range(chunks):
        rows = slice(c * q, (c + 1) * q)
        seg, _ = chunk_segments(starts_ref, base_ref, n, c, q)
        own, prev = seg[HALO:], seg[HALO - 1 : HALO]
        cum = cum_ref[0, rows]
        last = cum[q - 1 : q]
        ent = jnp.where(own == prev, jnp.exp(cum), 0.0)
        fade = jnp.where(own == own[q - 1 : q], jnp.exp(last - cum), 0.0)
        decay = jnp.where(own[q - 1 : q] == prev, jnp.exp(last), 0.0)
        prepared.append((ent, fade, decay, state))
        if c + 1 < chunks:
            tail = fade * step_ref[0, rows]
            b_low = act_ref[0, rows, wide : wide + LANES]
            gained = [
                dot(
                    b_low,
                    (
                        act_ref[0, rows, j * LANES : (j + 1) * LANES].astype(f32)
                        * pair_lanes(tail, j)
                    ).astype(bf16),
                    0,
                    0,
                )
                for j in range(pairs)
            ]
            state = expand(decay, pairs) * state + jnp.concatenate(gained, axis=1)

    dhead_ref[0] = jnp.zeros(dhead_ref.shape[1:], f32)
    dz_ref[:, :HALO] = jnp.zeros((groups, HALO, LANES), f32)
    dz_ref[:, HALO + length :] = jnp.zeros((groups, 8, LANES), f32)
    draw_ref[0, :HALO, groups * LANES :] = jnp.zeros((HALO, LANES), bf16)
    grad = leave_ref[0].astype(f32)
    for c in reversed(range(chunks)):
        rows = slice(c * q, (c + 1) * q)
        at = slice(HALO + c * q, HALO + (c + 1) * q)
        ent, fade, decay, state = prepared[c]
        step = step_ref[0, rows]
        tail = fade * step
        b_low = act_ref[0, rows, wide : wide + LANES]
        c_low = act_ref[0, rows, wide + LANES : wide + 2 * LANES]
        state_low = state.astype(bf16)
        grad_low = grad.astype(bf16)
        db = dbc_ref[0, rows, :LANES].astype(f32)
        dc = dbc_ref[0, rows, LANES:].astype(f32)
        by_step, by_tail, by_ent, next_grad = [], [], [], []
        for j in range(pairs):
            lanes = slice(j * LANES, (j + 1) * LANES)
            x = act_ref[0, rows, lanes].astype(f32)
            dy = dy_ref[0, rows, lanes].astype(f32)
            dscaled = dscaled_ref[0, rows, lanes].astype(f32)
            dweighted = dot(b_low, grad_low[:, lanes])
            wide_tail = pair_lanes(tail, j)
            entered = (dy * pair_lanes(ent, j)).astype(bf16)
            dx = dscaled * pair_lanes(step, j) + skip_ref[0:1, lanes] * dy + dweighted * wide_tail
            dz_ref[j, at] = dx * slope_ref[0, rows, lanes].astype(f32)
            by_step.append((dscaled * x).astype(bf16))
            by_tail.append((dweighted * x).astype(bf16))
            by_ent.append((dy * dot(c_low, state_low[:, lanes])).astype(bf16))
            db = db + dot((x * wide_tail).astype(bf16), grad_low[:, lanes], 1, 1)
            dc = dc + dot(entered, state_low[:, lanes], 1, 1)
            next_grad.append(dot(c_low, entered, 0, 0))
        dz_ref[pairs, at] = db * slope_ref[0, rows, wide : wide + LANES].astype(f32)
        dz_ref[pairs + 1, at] = dc * slope_ref[0, rows, wide + LANES : wide + 2 * LANES].astype(f32)
        dtail = head_sum(jnp.concatenate(by_tail, axis=1))
        dent = head_sum(jnp.concatenate(by_ent, axis=1))
        moved = dtail * tail
        ddecay = head_sum(
            jnp.broadcast_to(jnp.sum(grad * state, axis=0, keepdims=True), (8, wide))
        )[:1]
        at_last = jnp.sum(moved, axis=0, keepdims=True) + ddecay * decay
        dcum = dcum_ref[0, rows] + dent * ent - moved
        dcum = dcum + jnp.where(iota((q, LANES), 0) == q - 1, at_last, 0.0)
        drates = exact_dot(upper, dcum)
        rate = hp_ref[1:2]
        dstep = head_sum(jnp.concatenate(by_step, axis=1)) + dtail * fade + drates * rate
        dt_raw = raw_ref[0, at, groups * LANES :].astype(f32)
        ddt = jnp.where(used, dstep * sigmoid(dt_raw + hp_ref[0:1]), 0.0)
        draw_ref[0, at, groups * LANES :] = ddt.astype(bf16)
        dhead_ref[0, 0:1] += jnp.sum(ddt, axis=0, keepdims=True)
        dhead_ref[0, 1:2] += jnp.sum(
            jnp.where(used, drates * (rate * step), 0.0), axis=0, keepdims=True
        )
        grad = expand(decay, pairs) * grad + jnp.concatenate(next_grad, axis=1)

    total = HALO + length
    places = base_ref[0] - HALO + iota((total + 8, LANES), 0)
    seg = segment(starts_ref, n, places)
    near = [seg[k : k + total] == seg[:total] for k in range(1, 4)]
    dconv_ref[0, 5:] = jnp.zeros((3, groups * LANES), f32)
    for g in range(groups):
        lanes = slice(g * LANES, (g + 1) * LANES)
        taps = cw_ref[:, lanes]
        raw = raw_ref[0, :, lanes].astype(f32)
        dz = dz_ref[g, :total]
        out = taps[3:4] * dz
        dconv_ref[0, 4:5, lanes] = jnp.sum(dz, axis=0, keepdims=True)
        dconv_ref[0, 3:4, lanes] = jnp.sum(dz * raw, axis=0, keepdims=True)
        for k in range(1, 4):
            shifted = jnp.where(near[k - 1], dz_ref[g, k : k + total], 0.0)
            out = out + taps[3 - k : 4 - k] * shifted
            dconv_ref[0, 3 - k : 4 - k, lanes] = jnp.sum(shifted * raw, axis=0, keepdims=True)
        draw_ref[0, :, lanes] = out.astype(bf16)


def per_sequence(shape):
    return pl.BlockSpec((1,) + shape[1:], lambda n, *_: (n, 0, 0))


def shared(shape):
    return pl.BlockSpec(shape, lambda n, *_: (0, 0))


def call(kernel, scalars, inputs, outputs, flops, scratch=(), grid=None, ins=None, outs=None):
    specs = [shared(a.shape) if a.ndim == 2 else per_sequence(a.shape) for a in inputs]
    moved = sum(a.size * a.dtype.itemsize for a in list(inputs) + list(outputs))
    return pl.pallas_call(
        kernel,
        out_shape=outputs,
        grid_spec=pltpu.PrefetchScalarGridSpec(
            num_scalar_prefetch=len(scalars),
            grid=grid or (outputs[0].shape[0],),
            in_specs=ins or specs,
            out_specs=outs or [per_sequence(o.shape) for o in outputs],
            scratch_shapes=list(scratch),
        ),
        cost_estimate=pl.CostEstimate(flops=flops, transcendentals=0, bytes_accessed=moved),
        interpret=INTERPRET,
    )(*scalars, *inputs)


def spread(*shape, dtype=f32):
    return jax.ShapeDtypeStruct(shape, dtype)


def after(value, *others):
    return lax.optimization_barrier((value,) + others)[0]


def is_small():
    return lax.axis_size("lo") == 2 and lax.axis_size("bx") == 2


def gather_pieces(rows, hold):
    if not is_small():
        return [lax.all_gather(rows, PLANE, axis=0, tiled=False)]
    across = lax.ppermute(rows, "bx", SWAP)
    beside = lax.ppermute(rows, "lo", SWAP)
    corner = lax.ppermute(rows, ("lo", "bx"), CROSS)
    half = jnp.stack([after(rows, hold), beside, across, corner])
    return [half, lax.ppermute(half, "core", SWAP)]


def gather_single(rows):
    if not is_small():
        got = lax.all_gather(rows, PLANE, axis=0, tiled=False)
        return [got[i] for i in range(got.shape[0])]
    near = [
        rows,
        lax.ppermute(rows, "lo", SWAP),
        lax.ppermute(rows, "bx", SWAP),
        lax.ppermute(rows, ("lo", "bx"), CROSS),
    ]
    return near + [lax.ppermute(near[i], "core", SWAP) for i in range(4)]


def gather_edges(pieces, rows):
    low = lax.axis_size("lo")
    high = lax.axis_size("hi")
    place = lax.axis_index("lo")
    used = len(pieces) // 2 if is_small() else len(pieces)
    edges = []
    for i in range(0, used, low):
        at = [pieces[i + k][-rows:] for k in range(low)]
        edge = at[0]
        if low == 2:
            edge = jnp.where(place == 1, at[0], at[1])
        edges.append(edge)
    route = tuple((i, i + 1) for i in range(high - 1))
    came = lax.ppermute(jnp.stack(edges), "hi", route)
    if is_small():
        came = jnp.concatenate([came, lax.ppermute(came, "core", SWAP)])
    return came


def scatter_pieces(make):
    if not is_small():
        sent = make(0, lax.axis_size("bx") * lax.axis_size("core"))
        return lax.psum_scatter(sent, PLANE, scatter_dimension=0, tiled=False).astype(f32)
    other = make(2, 2)
    came = lax.ppermute(other, "core", SWAP)
    own = make(0, 2)

    def piece(i):
        return own[i].astype(f32) + came[i].astype(f32)

    beside = lax.ppermute(piece(1).astype(bf16), "lo", SWAP)
    across = lax.ppermute(piece(2).astype(bf16), "bx", SWAP)
    corner = lax.ppermute(piece(3).astype(bf16), ("lo", "bx"), CROSS)
    return piece(0) + across.astype(f32) + beside.astype(f32) + corner.astype(f32)


def scatter_halves(make):
    if not is_small():
        return scatter_pieces(make)
    other = make(2, 2)
    came = lax.ppermute(other, "core", SWAP)
    own = make(0, 2)
    middle = own.shape[2] // 2
    left, right = slice(0, middle), slice(middle, 2 * middle)

    def piece(i, half):
        return own[i, :, half].astype(f32) + came[i, :, half].astype(f32)

    def pair(i, j, half):
        return jnp.stack([piece(i, half), piece(j, half)]).astype(bf16)

    by_x = lax.ppermute(pair(2, 3, left), "bx", SWAP)
    by_y = lax.ppermute(pair(1, 3, right), "lo", SWAP)
    last_y = lax.ppermute((piece(1, left) + by_x[1].astype(f32)).astype(bf16), "lo", SWAP)
    last_x = lax.ppermute((piece(2, right) + by_y[1].astype(f32)).astype(bf16), "bx", SWAP)
    return jnp.concatenate(
        [
            piece(0, left) + by_x[0].astype(f32) + last_y.astype(f32),
            piece(0, right) + by_y[0].astype(f32) + last_x.astype(f32),
        ],
        axis=1,
    )


def sum_plane(stats):
    if not is_small():
        return lax.psum(stats, PLANE)
    rest = stats.shape[1:]
    grid = stats.reshape((2, 2) + rest)
    grid = grid + lax.ppermute(grid[::-1], "core", SWAP)
    grid = grid + lax.ppermute(grid[:, ::-1], "bx", SWAP)
    grid = grid + lax.ppermute(grid, "lo", SWAP)
    return grid.reshape(stats.shape)


def gather_starts(starts):
    if not is_small():
        return lax.all_gather(starts, ("bx", "core"), axis=0, tiled=True)
    half = jnp.concatenate([starts, lax.ppermute(starts, "bx", SWAP)])
    return jnp.concatenate([half, lax.ppermute(half, "core", SWAP)])


def piece_of(low, offset=0):
    def index(n, p, place):
        return (low * n + (p ^ place[0]) - offset, 0, 0)

    return index


def half_specs(halves, shape, low):
    count = halves[0].shape[0]
    specs = []
    for h in range(len(halves)):

        def index(n, p, place, h=h):
            return (jnp.clip(low * n + (p ^ place[0]) - h * count, 0, count - 1), 0, 0)

        specs.append(pl.BlockSpec((1,) + shape, index))
    return specs


def chain(state, decay, forward):
    size = lax.axis_size("hi")
    place = lax.axis_index("hi")
    enter = jnp.zeros(state.shape, bf16)
    for k in range(size - 1):
        source = k if forward else size - 1 - k
        target = source + 1 if forward else source - 1
        passed = (state + decay * enter.astype(f32)).astype(bf16)
        came = lax.ppermute(passed, "hi", ((source, target),))
        enter = jnp.where(place == target, came, enter)
    return enter


def to_shards(columns, width):
    low = lax.axis_size("lo")
    batch = lax.axis_size("bx") * lax.axis_size("core")
    rows = columns.shape[0]
    split = columns.reshape(rows, batch, low, width)
    return jnp.transpose(split, (2, 1, 0, 3)).reshape(low * batch, rows, width)


def from_shards(blocks):
    low = lax.axis_size("lo")
    batch = lax.axis_size("bx") * lax.axis_size("core")
    _, rows, width = blocks.shape
    split = blocks.reshape(low, batch, rows, width)
    return jnp.transpose(split, (2, 1, 0, 3)).reshape(rows, batch * low * width)


def exchange(blocks, axes=PLANE):
    return lax.all_to_all(blocks, axes, 0, 0, tiled=True)


def step_of(
    residual_in,
    seg_ids,
    doc_starts,
    norm_gain,
    in_weight,
    conv_weight,
    conv_bias,
    dt_bias,
    a_log,
    skip_weight,
    gate_gain,
    out_weight,
    cotangent,
):
    high, low = lax.axis_size("hi"), lax.axis_size("lo")
    batch = lax.axis_size("bx") * lax.axis_size("core")
    team = low * batch
    devices = high * team
    row_count, features = residual_in.shape[1:]
    heads = dt_bias.shape[0] // team
    inner = gate_gain.shape[0] * devices
    channels = conv_bias.shape[0] * devices
    width = inner // team
    shared_width = channels - inner
    taps = conv_weight.shape[1]
    length = low * row_count
    q = row_count
    total = HALO + length
    pad_width = width + shared_width + LANES
    at_dt = width + shared_width
    k_rows = in_weight.shape[0]
    o_rows = out_weight.shape[0]
    sequences = batch
    place_low = lax.axis_index("lo")
    place_batch = lax.axis_index("bx") * lax.axis_size("core") + lax.axis_index("core")
    shard = place_batch * low + place_low
    place = place_low.reshape(1).astype(jnp.int32)
    base = (lax.axis_index("hi") * length).reshape(1).astype(jnp.int32)

    lanes_of = conv_bias.shape[0]
    small = jnp.stack(
        [conv_weight[:, k] for k in range(taps)]
        + [conv_bias]
        + [jnp.pad(gain, (0, lanes_of - gain.shape[0])) for gain in (gate_gain, norm_gain)]
    )
    small = jnp.pad(small, ((0, 8 - taps - 3), (0, LANES - lanes_of))).reshape(-1)
    small_lanes = -(-small.shape[0] // k_rows)
    small = jnp.pad(small, (0, small_lanes * k_rows - 8 * LANES)).reshape(k_rows, small_lanes)
    at_small = at_dt + heads
    block = jnp.concatenate(
        [
            to_shards(in_weight[:, inner : 2 * inner], width),
            jnp.broadcast_to(
                in_weight[:, 2 * inner : inner + channels], (team, k_rows, shared_width)
            ),
            to_shards(in_weight[:, inner + channels :], heads),
            jnp.broadcast_to(small, (team, k_rows, small_lanes)),
            jnp.zeros((team, k_rows, pad_width - at_small - small_lanes), bf16),
        ],
        axis=2,
    )
    rows_of_plane = exchange(block)
    small = rows_of_plane[:, :, at_small : at_small + small_lanes].reshape(team, -1)
    small = small[:, : 8 * LANES].reshape(team, 8, LANES)
    rows_of_plane = rows_of_plane.reshape(team * k_rows, pad_width)
    conv_w = lax.all_gather(rows_of_plane, "hi", axis=0, tiled=True)

    resid = gather_single(after(residual_in[0], rows_of_plane))
    starts = gather_starts(after(doc_starts, rows_of_plane))
    halo = gather_edges(resid, HALO)

    small = lax.all_gather(small, "hi", axis=0, tiled=False).reshape(devices, 8, LANES)
    small = jnp.swapaxes(small.astype(f32), 0, 1)
    table = small[: taps + 1, :, :lanes_of].reshape(taps + 1, channels)
    full_gate = small[taps + 1, :, : gate_gain.shape[0]].reshape(1, inner)
    full_gain = small[taps + 2, :, : norm_gain.shape[0]].reshape(1, features)
    cw = jnp.concatenate(
        [lax.dynamic_slice_in_dim(table, shard * width, width, 1), table[:, inner:]], axis=1
    )
    cw = jnp.pad(cw, ((0, 8 - taps - 1), (0, 0)))
    gain_row = jnp.broadcast_to(
        lax.dynamic_slice_in_dim(full_gate, shard * width, width, 1), (8, width)
    )
    own_head = functools.partial(
        lax.dynamic_slice_in_dim, start_index=shard * heads, slice_size=heads
    )
    hp = jnp.stack([own_head(dt_bias), -jnp.exp(own_head(a_log))])
    hp = jnp.pad(hp, ((0, 6), (0, LANES - heads)))
    skip_row = jnp.broadcast_to(jnp.repeat(own_head(skip_weight), width // heads), (8, width))

    sub = features // width
    gate_block = exchange(after(to_shards(in_weight[:, :inner], width), rows_of_plane))
    gate_block = gate_block.reshape(sub, -1, width)
    gate_block = jnp.concatenate([gate_block[i] for i in range(sub)], axis=1)
    gate_rows_count = gate_block.shape[0]
    second = lax.all_gather(
        jnp.concatenate([gate_block, out_weight]), "hi", axis=0, tiled=False
    )

    norm_row = jnp.broadcast_to(full_gain, (8, features))
    (normed,) = call(
        functools.partial(norm_rows, low=low, slots=sequences),
        (place,),
        [halo, norm_row] + resid,
        (spread(sequences, total, features, dtype=bf16),),
        sequences * total * features * 10,
    )
    flat = normed.reshape(-1, features)
    raw = dot(flat, conv_w).astype(bf16).reshape(sequences, total, pad_width)

    act_shape = (sequences, length, width + shared_width)
    wide_shape = (sequences, length, width)
    col_shape = (sequences, length, LANES)
    row_shape = (sequences, 8, length)
    state_shape = (sequences, shared_width // 2, width)
    unit = sequences * length * width
    act, slope, y_local, ent, step, cum, cum_r, state, decay = call(
        functools.partial(scan_forward, heads=heads, q=q),
        (starts, base),
        (raw, cw, hp, skip_row),
        (
            spread(*act_shape, dtype=bf16),
            spread(*act_shape, dtype=bf16),
            spread(*wide_shape, dtype=bf16),
            spread(*col_shape),
            spread(*col_shape),
            spread(*col_shape),
            spread(*row_shape),
            spread(*state_shape),
            spread(sequences, 8, width),
        ),
        unit * 8 * q,
        scratch=(pltpu.VMEM((at_dt // LANES, HALO + q, LANES), f32),),
    )
    cot = gather_pieces(after(cotangent[0], normed), state)
    split = sequences // len(cot)
    decay = decay[:, :1]
    enter = chain(state, decay, True)

    gate_w = jnp.concatenate(
        [
            second[:, None, :gate_rows_count, i * width : (i + 1) * width]
            for i in range(sub)
        ],
        axis=1,
    ).reshape(features, width)
    gate = dot(flat, gate_w).astype(bf16).reshape(sequences, total, width)
    out_w = second[:, gate_rows_count:]
    out_w = exchange(out_w, ("bx", "core")).reshape(batch, high // batch, o_rows, features)
    out_w = jnp.swapaxes(out_w, 0, 1).reshape(width, features)
    u = [
        dot(half.reshape(-1, features), out_w, 1, 1).astype(bf16).reshape(-1, row_count, width)
        for half in cot
    ]

    def chunk(lanes):
        return pl.BlockSpec((1, q, lanes), lambda n, p, place: (n, p, 0))

    def whole(rows, lanes):
        return pl.BlockSpec((1, rows, lanes), lambda n, p, place: (n, 0, 0))

    def fixed(a):
        return pl.BlockSpec(a.shape, lambda n, p, place: (0, 0))

    across = pl.BlockSpec((1, 8, q), lambda n, p, place: (n, 0, p))
    states = whole(*state_shape[1:])
    u_specs = half_specs(cot, (row_count, width), low)
    grid = (sequences, low)
    y, stats, unscaled = call(
        functools.partial(gate_forward, heads=heads, q=q, split=split),
        (place,),
        [y_local, ent, act, enter, gate, gain_row] + u,
        (
            spread(*wide_shape, dtype=bf16),
            spread(*row_shape),
            spread(team, row_count, width, dtype=bf16),
        ),
        unit * 300,
        grid=grid,
        ins=[
            chunk(width),
            chunk(LANES),
            chunk(width + shared_width),
            states,
            whole(total, width),
            fixed(gain_row),
        ]
        + u_specs,
        outs=[chunk(width), across, pl.BlockSpec((1, q, width), piece_of(low))],
    )
    stats = sum_plane(stats)
    my_slot = 0 if is_small() else place_batch

    def mixed_pieces(first, slots):
        rows = unscaled[first * low : (first + slots) * low].reshape(-1, width)
        return dot(rows, out_w).astype(bf16).reshape(-1, row_count, features)

    mixed = scatter_pieces(mixed_pieces)
    own_squares = lax.dynamic_slice_in_dim(stats[my_slot, 0], place_low * row_count, row_count)
    mixed_scale = lax.rsqrt(own_squares / inner + epsilon)[:, None]
    mixed_out = (residual_in[0].astype(f32) + mixed_scale * mixed).astype(bf16)

    dy, dgate, mixer_low, enter_grad, gate_sums = call(
        functools.partial(gate_backward, heads=heads, q=q, columns=inner, split=split),
        (place,),
        [y, ent, act, gate, gain_row, stats] + u,
        (
            spread(*wide_shape, dtype=bf16),
            spread(sequences, total, width, dtype=bf16),
            spread(team, row_count, width, dtype=bf16),
            spread(*state_shape),
            spread(sequences, 8, width),
        ),
        unit * 300,
        grid=grid,
        ins=[
            chunk(width),
            chunk(LANES),
            chunk(width + shared_width),
            whole(total, width),
            fixed(gain_row),
            across,
        ]
        + u_specs,
        outs=[
            chunk(width),
            whole(total, width),
            pl.BlockSpec((1, q, width), piece_of(low)),
            states,
            whole(8, width),
        ],
    )
    leave = chain(enter_grad, decay, False)
    gate_sums = jnp.sum(gate_sums, axis=0)
    dskip = jnp.sum(gate_sums[1].reshape(heads, -1), axis=1)
    gain_all = lax.dynamic_update_slice(
        jnp.zeros((1, inner), f32), gate_sums[:1], (0, shard * width)
    )

    count = cot[0].shape[0]
    out_grad = 0.0
    for h, half in enumerate(cot):
        rows = mixer_low[h * count : (h + 1) * count].reshape(-1, width)
        out_grad = out_grad + dot(rows, half.reshape(-1, features), 0, 0)
    out_grad = out_grad.astype(bf16).reshape(high // batch, batch, o_rows, features)
    out_grad = exchange(
        jnp.swapaxes(out_grad, 0, 1).reshape(high, o_rows, features), ("bx", "core")
    )
    dgate_flat = dgate.reshape(-1, width)
    gate_grad = dot(flat, dgate_flat, 0, 0).astype(bf16)
    gate_grad = gate_grad.reshape(high, sub, gate_rows_count, width)
    gate_grad = jnp.concatenate([gate_grad[:, i] for i in range(sub)], axis=2)
    early = jnp.concatenate([gate_grad, out_grad], axis=1)
    early = lax.psum_scatter(early, "hi", scatter_dimension=0, tiled=False)

    def piecewise(lanes):
        return pl.BlockSpec((1, q, lanes), lambda n, p, *_: (n, p, 0))

    dscaled, dbc, dcum = call(
        functools.partial(scan_backward_inner, heads=heads, q=q),
        (starts, base),
        (act, dy, step, cum, cum_r),
        (
            spread(*wide_shape, dtype=bf16),
            spread(sequences, length, shared_width, dtype=bf16),
            spread(*col_shape),
        ),
        unit * 16 * q,
        grid=grid,
        ins=[piecewise(a.shape[2]) for a in (act, dy, step, cum)]
        + [pl.BlockSpec((1, 8, q), lambda n, p, *_: (n, 0, p))],
        outs=[piecewise(width), piecewise(shared_width), piecewise(LANES)],
    )
    draw, dconv, dhead = call(
        functools.partial(scan_backward_outer, heads=heads, q=q),
        (starts, base),
        (raw, act, slope, dy, step, cum, dscaled, dbc, dcum, enter, leave, cw, hp, skip_row),
        (
            spread(sequences, total, pad_width, dtype=bf16),
            spread(sequences, 8, width + shared_width),
            spread(sequences, 8, LANES),
        ),
        unit * 2000,
        scratch=(pltpu.VMEM((at_dt // LANES, total + 8, LANES), f32),),
    )
    draw_flat = draw.reshape(-1, pad_width)

    edge_rows = draw[:, :HALO].reshape(-1, pad_width)
    returned = lax.ppermute(
        dot(edge_rows, conv_w, 1, 1).astype(bf16).reshape(sequences, HALO, features),
        "hi",
        tuple((i + 1, i) for i in range(high - 1)),
    )

    late = dot(flat, draw_flat, 0, 0).astype(bf16)
    dconv = jnp.sum(dconv, axis=0)
    dhead = jnp.sum(dhead, axis=0)

    def placed(mine, size):
        return lax.dynamic_update_slice(
            jnp.zeros((mine.shape[0], size), f32), mine, (0, shard * mine.shape[1])
        )

    by_owner = jnp.concatenate(
        [placed(dconv[: taps + 1, :width], inner), dconv[: taps + 1, width:]], axis=1
    ).reshape(taps + 1, devices, lanes_of)
    heads_all = placed(jnp.concatenate([dhead[:2, :heads], dskip[None]]), heads * team)
    spare = pad_width - at_dt - heads

    def rows_for_owners(array):
        array = jnp.broadcast_to(array, (array.shape[0], devices, array.shape[2]))
        return jnp.pad(array, ((0, 0), (0, 0), (0, spare - array.shape[2])))

    spare_rows = jnp.concatenate(
        [
            rows_for_owners(by_owner),
            rows_for_owners(gain_all.reshape(1, devices, -1)),
            rows_for_owners(heads_all[:, None]),
        ]
    )
    spare_rows = jnp.swapaxes(spare_rows, 0, 1)
    spare_rows = jnp.pad(spare_rows, ((0, 0), (0, k_rows - spare_rows.shape[1]), (0, 0)))
    spare_rows = spare_rows.reshape(devices * k_rows, spare).astype(bf16)
    late = jnp.concatenate([late[:, : at_dt + heads], spare_rows], axis=1)
    late_sum = lax.psum_scatter(late, "hi", scatter_dimension=0, tiled=True)

    def grad_pieces(first, slots):
        def slot(n, p, place):
            return (n + first, 0, 0)

        (out,) = call(
            functools.partial(normed_backward, q=q),
            (place,),
            (draw, dgate, returned, conv_w, gate_w),
            (spread(slots * low, row_count, features, dtype=bf16),),
            2 * slots * length * features * (pad_width + width),
            grid=(slots, low),
            ins=[
                pl.BlockSpec((1, total, pad_width), slot),
                pl.BlockSpec((1, total, width), slot),
                pl.BlockSpec((1, HALO, features), slot),
                fixed(conv_w),
                fixed(gate_w),
            ],
            outs=[pl.BlockSpec((1, q, features), piece_of(low))],
        )
        return out

    own_grad = scatter_halves(grad_pieces)
    own_grad = own_grad * full_gain
    own = residual_in[0].astype(f32)
    own_scale = lax.rsqrt(jnp.mean(own * own, axis=-1, keepdims=True) + epsilon)
    unit_rows = own * own_scale
    along = jnp.mean(own_grad * unit_rows, axis=-1, keepdims=True)
    input_grad = cotangent[0].astype(f32) + own_scale * (own_grad - unit_rows * along)

    gate_share = jnp.concatenate(
        [early[None, :gate_rows_count, i * width : (i + 1) * width] for i in range(sub)]
    )
    gate_share = exchange(gate_share.reshape(team, k_rows, width))
    gate_share = from_shards(gate_share).astype(f32)
    out_share = early[gate_rows_count:].astype(f32)
    late_share = exchange(late_sum.reshape(team, k_rows, pad_width)).astype(f32)
    summed = jnp.sum(late_share[:, :, width:], axis=0)
    little = summed[:, shared_width + heads :]
    in_share = jnp.concatenate(
        [
            gate_share,
            from_shards(late_share[:, :, :width]),
            summed[:, :shared_width],
            from_shards(late_share[:, :, at_dt : at_dt + heads]),
        ],
        axis=1,
    )
    norm_share = jnp.sum(in_share * in_weight.astype(f32), axis=1) / norm_gain.astype(f32)
    return (
        mixed_out[None],
        input_grad[None],
        norm_share,
        in_share,
        little[:taps, :lanes_of].T,
        little[taps, :lanes_of],
        little[taps + 2, : heads * team],
        little[taps + 3, : heads * team],
        little[taps + 4, : heads * team],
        little[taps + 1, : gate_gain.shape[0]],
        out_share,
    )


def solution(mesh):
    seq, batch = mesh.shape["seq"], mesh.shape["batch"]
    low = max(1, 8 // batch)
    split = Mesh(
        mesh.devices.reshape(seq // low, low, batch // 2, 2), ("hi", "lo", "bx", "core")
    )
    everything = ("hi", "lo", "bx", "core")
    batches, blocks = ("bx", "core"), ("hi", "lo")
    rows = P(batches, blocks, None)
    return jax.shard_map(
        step_of,
        mesh=split,
        in_specs=(
            rows,
            P(batches, blocks),
            P(batches, None),
            P(everything),
            P(everything, None),
            P(everything, None),
            P(everything),
            P(),
            P(),
            P(),
            P(everything),
            P(everything, None),
            rows,
        ),
        out_specs=(
            rows,
            rows,
            P(everything),
            P(everything, None),
            P(everything, None),
            P(everything),
            P(),
            P(),
            P(),
            P(everything),
            P(everything, None),
        ),
        check_vma=False,
    )
```
